32 devices in a mesh: sta: 16 (over z, y, core), band: 2 (over x).
Axes of the slice: x: 2, y: 2, z: 4, core: 2. Of those that a mesh axis runs over, the one named last changes fastest.
Arguments:
- traces: bfloat16 [64, 8, 16384], P('sta', 'band'), may hold values from -400 to 400, as said below
- live_flag: int32 [64, 8], P('sta'), may hold values 0 or 1
- response: float32 [8192], P('band'), may hold values from 0.3 to 3
Outputs:
- own_cross: bfloat16 [2, 64, 4, 8192], P(None, 'sta', None, 'band')
- near_cross: bfloat16 [2, 64, 4, 8192], P(None, 'sta', None, 'band')
- far_cross: bfloat16 [2, 64, 4, 8192], P(None, 'sta', None, 'band')
The draws below stay inside these ranges and needn't reach their ends.
Inputs may be any that keep to these rules, and one draw needn't show every extreme that they name: `traces`: recorded ground motion of each station and window.
All inputs are finite; a program needn't handle non-finite values. No bound on the sum of `live_flag` on one device may be relied on, other than what follows from the above.
Results may differ from the reference program's by a relative error of at most 0.008.
Values may be sent and summed in bfloat16 or wider, within the bound.
No kernel may reach another device: no remote copies, remote signals or barrier semaphores. Data moves between devices by JAX's collectives and lax.ppermute only.
A program may use at most 64 MiB of HBM per device.

```python
import math
import jax
import jax.numpy as jnp
from jax import lax

ST_DEV = 4
ROOT = 128
SMOOTH = 64
STATIONS = 64
WINDOWS = 8
SAMPLES = 16384
BINS = 8192
NEAR = 2
N_STA = 16


def draw_traces(key, part):
    keys = jax.random.split(key, 6)
    times = jnp.arange(SAMPLES, dtype=jnp.int32)
    tones = jax.random.randint(keys[0], (64,), 1, SAMPLES // 2)
    phases = jax.random.uniform(keys[1], (WINDOWS, 64), minval=-math.pi, maxval=math.pi)
    turns = tones[:, None] * times[None, :] % SAMPLES
    waves = jnp.cos(turns.astype(jnp.float32)[None, :, :] * (2.0 * math.pi / SAMPLES) + phases[:, :, None])
    signal = 0.15 * jnp.sum(waves, axis=1)
    coupling = jax.random.uniform(keys[2], (STATIONS, 1, 1), minval=0.5, maxval=1.5)
    noise = jnp.clip(jax.random.normal(keys[3], (STATIONS, WINDOWS, SAMPLES)), -6.0, 6.0)
    gains = jnp.exp(jax.random.uniform(keys[5], (STATIONS, WINDOWS, 1), minval=0.0, maxval=math.log(10.0)))
    return (gains * (noise + coupling * signal[None, :, :])).astype(jnp.bfloat16)


def place_ends(drawn, rng, least, high):
    spot = [jax.random.randint(jax.random.fold_in(rng, axis), (), 0, length) for axis, length in enumerate(drawn.shape)]
    widest = drawn.shape.index(max(drawn.shape))
    beside = spot[:widest] + [(spot[widest] + 1) % drawn.shape[widest]] + spot[widest + 1:]
    return drawn.at[tuple(spot)].set(least).at[tuple(beside)].set(high)


def levels(key, shape, shards, low, high):
    factor_of, own = 1.0, jax.random.fold_in(key, 6)
    for position, shards_of in shards:
        steps = jnp.exp(jax.random.uniform(jax.random.fold_in(own, position), (shards_of,), jnp.float32, low / len(shards), high / len(shards)))
        factor_of = factor_of * jnp.repeat(steps, shape[position] // shards_of).reshape([-1 if axis == position else 1 for axis in range(len(shape))])
    return factor_of


def setup_inputs(seed: int = 0) -> dict:
    arg_keys = jax.random.split(jax.random.key(seed), 4)
    return {
        "traces": draw_traces(jax.random.fold_in(arg_keys[3], 71), 0),
        "live_flag": place_ends((jax.random.randint(arg_keys[1], (STATIONS, WINDOWS), 0, 4) < 3).astype(jnp.int32), jax.random.fold_in(arg_keys[1], 1), 0, 1),
        "response": jnp.clip(jnp.exp(math.log(3.0) - 2.3025851 * jax.random.uniform(arg_keys[2], (BINS,), jnp.float32) ** levels(arg_keys[2], (BINS,), ((0, 2),), -0.2, 0.2)), 0.3, 3.0),
    }


epsilon = 1e-06
full_turn = 2.0 * math.pi

def make_tables():
    indices = jnp.arange(ROOT, dtype=jnp.int32)
    products = indices[:, None] * indices[None, :] % ROOT
    angles = products.astype(jnp.float32) * (full_turn / ROOT)
    first_table = jnp.concatenate([jnp.cos(angles), -jnp.sin(angles)], axis=1).astype(jnp.bfloat16)
    twist_angle = (indices[:, None] * indices[None, :]).astype(jnp.float32) * (full_turn / (ROOT * ROOT))
    twist_cos = jnp.cos(twist_angle)
    twist_sin = jnp.sin(twist_angle)
    half_angle = angles[:, :ROOT // 2]
    cos_part = jnp.cos(half_angle)
    sin_part = jnp.sin(half_angle)
    second_table = jnp.stack([jnp.stack([cos_part, -sin_part], axis=1), jnp.stack([sin_part, cos_part], axis=1)], axis=0).astype(jnp.bfloat16)
    return (first_table, twist_cos, twist_sin, second_table)

def transform(block, tables):
    first_table, twist_cos, twist_sin, second_table = tables
    station_rows, window_rows = (block.shape[0], block.shape[1])
    folded = block.reshape(station_rows, window_rows, ROOT, ROOT).astype(jnp.float32)
    section_one = jnp.einsum('swab,ak->swbk', folded, first_table.astype(jnp.float32))
    real_one = section_one[..., :ROOT]
    imag_one = section_one[..., ROOT:]
    real_two = real_one * twist_cos + imag_one * twist_sin
    imag_two = imag_one * twist_cos - real_one * twist_sin
    twisted = jnp.stack([real_two, imag_two], axis=2).astype(jnp.bfloat16)
    result = jnp.einsum('swcbk,cbeq->sweqk', twisted.astype(jnp.float32), second_table.astype(jnp.float32))
    return result.astype(jnp.bfloat16).reshape(station_rows, window_rows, 2, ROOT // 2 * ROOT)

def cross_spectra(left, right):
    left_wide = left.astype(jnp.float32)
    right_wide = right.astype(jnp.float32)
    real_part = jnp.einsum('iwcf,jwcf->ijf', left_wide, right_wide)
    imag_part = jnp.einsum('iwf,jwf->ijf', left_wide[:, :, 1], right_wide[:, :, 0]) - jnp.einsum('iwf,jwf->ijf', left_wide[:, :, 0], right_wide[:, :, 1])
    return (jnp.stack([real_part, imag_part], axis=0) / WINDOWS).astype(jnp.bfloat16)

def reference(traces, live_flag, response):
    tables = make_tables()
    blocks = traces.reshape(N_STA, ST_DEV, WINDOWS, SAMPLES)
    gate_blocks = live_flag.astype(jnp.float32).reshape(N_STA, ST_DEV, WINDOWS)

    def whiten(pair_item):
        block, gates = pair_item
        masked = transform(block, tables).astype(jnp.float32) * gates[:, :, None, None]
        power_sum = lax.optimization_barrier(jnp.sum(masked[:, :, 0, :] ** 2 + masked[:, :, 1, :] ** 2, axis=1))
        padded = jnp.pad(power_sum, ((0, 0), (SMOOTH, SMOOTH)))
        window_sum = lax.reduce_window(padded, jnp.zeros((), padded.dtype), lax.add, (1, 2 * SMOOTH + 1), (1, 1), 'VALID')
        smooth = window_sum / ((2 * SMOOTH + 1) * WINDOWS)
        scales = response[None, :] / jnp.sqrt(smooth + epsilon)
        return (masked * scales[:, None, None, :]).astype(jnp.bfloat16)
    whitened = lax.map(whiten, (blocks, gate_blocks))

    def pairs(block_index):
        own_block = lax.dynamic_index_in_dim(whitened, block_index, 0, keepdims=False)
        near_index = ((block_index + NEAR) % N_STA).astype(jnp.int32)
        far_index = ((block_index + 2 * NEAR) % N_STA).astype(jnp.int32)
        near_block = lax.dynamic_index_in_dim(whitened, near_index, 0, keepdims=False)
        far_block = lax.dynamic_index_in_dim(whitened, far_index, 0, keepdims=False)
        return (cross_spectra(own_block, own_block), cross_spectra(own_block, near_block), cross_spectra(own_block, far_block))
    results = lax.map(pairs, jnp.arange(N_STA, dtype=jnp.int32))

    def arrange(stacked):
        return jnp.transpose(stacked, (1, 0, 2, 3, 4)).reshape(2, STATIONS, ST_DEV, BINS)
    return (arrange(results[0]), arrange(results[1]), arrange(results[2]))
```

```python
import functools
import math

import jax
import jax.numpy as jnp
import numpy as np
from jax import lax
from jax.experimental import pallas as pl
from jax.experimental.pallas import tpu as pltpu
from jax.sharding import PartitionSpec as P

ROOT = 128
SMOOTH = 64
epsilon = 1e-06


@functools.cache
def tables():
    n = np.arange(ROOT)
    angle = 2.0 * math.pi * ((n[:, None] * n[None, :]) % ROOT) / ROOT
    first = np.concatenate([np.cos(angle), -np.sin(angle)], axis=1)
    twist = 2.0 * math.pi * (n[:, None] * n[None, :]) / (ROOT * ROOT)
    half = angle[:, : ROOT // 2]
    c, s = np.cos(half), np.sin(half)
    second = np.concatenate(
        [np.concatenate([c, -s], axis=1), np.concatenate([s, c], axis=1)], axis=0
    )
    return (
        jnp.asarray(first.T, jnp.bfloat16),
        jnp.asarray(np.cos(twist), jnp.float32),
        jnp.asarray(np.sin(twist), jnp.float32),
        jnp.asarray(second.T, jnp.bfloat16),
    )


@functools.cache
def smoother():
    src = np.arange(3 * ROOT)[:, None] - ROOT
    dst = np.arange(ROOT)[None, :]
    return jnp.asarray(np.abs(src - dst) <= SMOOTH, jnp.bfloat16)


def transform_kernel(
    band_ref, flag_ref, x_ref, first_ref, cos_ref, sin_ref, second_ref, *refs,
    stations, windows, bands,
):
    outs, (wide, full, edges) = refs[:bands], refs[bands:]
    rows = ROOT // 2 // bands
    here = band_ref[0]
    lane = lax.broadcasted_iota(jnp.int32, (1, ROOT), 1)
    for s in range(stations):
        wide[...] = x_ref[s].astype(jnp.float32)
        folded = jnp.concatenate(
            [
                wide[pl.ds(w, ROOT, stride=windows), :].astype(jnp.bfloat16)
                for w in range(windows)
            ],
            axis=1,
        )
        one = jnp.dot(first_ref[...], folded, preferred_element_type=jnp.float32)
        for w in range(windows):
            real = one[:ROOT, w * ROOT : (w + 1) * ROOT]
            imag = one[ROOT:, w * ROOT : (w + 1) * ROOT]
            turned = jnp.concatenate(
                [
                    real * cos_ref[...] + imag * sin_ref[...],
                    imag * cos_ref[...] - real * sin_ref[...],
                ],
                axis=1,
            ).astype(jnp.bfloat16)
            two = lax.dot_general(
                second_ref[...], turned, (((1,), (1,)), ((), ())),
                preferred_element_type=jnp.float32,
            )
            gate = flag_ref[s, here * windows + w].astype(jnp.float32)
            full[...] = two * gate
            at = s * windows + w
            for k in range(bands):
                band = lax.rem(here + k, bands)
                start = pl.multiple_of(band * rows, 8)
                halves = []
                for e in range(2):
                    base = e * (ROOT // 2)
                    halves.append(full[pl.ds(base + start, rows), :])
                    after = full[pl.ds(base + jnp.minimum(start + rows, ROOT // 2 - 1), 1), :]
                    before = full[pl.ds(base + jnp.maximum(start - 1, 0), 1), :]
                    after = jnp.where(band == bands - 1, 0.0, after)
                    before = jnp.where(band == 0, 0.0, before)
                    edges[k, pl.ds(2 * at + e, 1), :] = jnp.where(lane < SMOOTH, after, before)
                outs[k][pl.ds(2 * at * rows, 2 * rows), :] = jnp.concatenate(
                    halves, axis=0
                ).astype(jnp.bfloat16)
    body = 2 * stations * windows * rows
    for k in range(bands):
        outs[k][pl.ds(body, 2 * stations * windows), :] = edges[k].astype(jnp.bfloat16)


def transform(traces, live_flag, bands):
    stations, windows, samples = traces.shape
    packed = traces.reshape(stations, windows, ROOT, ROOT).transpose(0, 2, 1, 3)
    packed = packed.reshape(stations, ROOT * windows, ROOT)
    rows = ROOT // 2 // bands
    height = 2 * stations * windows * (rows + 1)
    band = lax.axis_index("band").astype(jnp.int32).reshape(1)
    smem = pl.BlockSpec(memory_space=pltpu.SMEM)
    vmem = pl.BlockSpec(memory_space=pltpu.VMEM)
    return pl.pallas_call(
        functools.partial(transform_kernel, stations=stations, windows=windows, bands=bands),
        out_shape=[jax.ShapeDtypeStruct((height, ROOT), jnp.bfloat16)] * bands,
        in_specs=[smem, smem] + [vmem] * 5,
        out_specs=[vmem] * bands,
        scratch_shapes=[
            pltpu.VMEM((ROOT * windows, ROOT), jnp.float32),
            pltpu.VMEM((ROOT, ROOT), jnp.float32),
            pltpu.VMEM((bands, 2 * stations * windows, ROOT), jnp.float32),
        ],
        name="transform",
    )(band, live_flag, packed, *tables())


def block_scales(chunks, gain, window, stations, windows, rows):
    body = 2 * stations * windows * rows
    total = len(chunks) * windows
    parts = []
    for s in range(stations):
        power = jnp.zeros((rows, ROOT), jnp.float32)
        edge = jnp.zeros((1, ROOT), jnp.float32)
        for chunk in chunks:
            for w in range(windows):
                at = 2 * (s * windows + w)
                cell = chunk[pl.ds(at * rows, 2 * rows), :].astype(jnp.float32)
                power = power + cell[:rows] * cell[:rows] + cell[rows:] * cell[rows:]
        parts.append(power)
    edges = []
    for chunk in chunks:
        line = chunk[pl.ds(body, 2 * stations * windows), :].astype(jnp.float32)
        edges.append(line * line)
    edges = sum(edges[1:], edges[0])
    rows_of = []
    for s in range(stations):
        span = 2 * windows
        edge = jnp.sum(edges[s * span : (s + 1) * span], axis=0, keepdims=True)
        power = parts[s]
        before = jnp.concatenate([edge, power[:-1]], axis=0)
        after = jnp.concatenate([power[1:], edge], axis=0)
        rows_of.append(jnp.concatenate([before, power, after], axis=1))
    spread = jnp.concatenate(rows_of, axis=0)
    high = spread.astype(jnp.bfloat16)
    rest = spread - high.astype(jnp.float32)
    middle = rest.astype(jnp.bfloat16)
    low = (rest - middle.astype(jnp.float32)).astype(jnp.bfloat16)
    smooth = sum(
        jnp.dot(part, window, preferred_element_type=jnp.float32) for part in (low, middle, high)
    ) / ((2 * SMOOTH + 1) * total)
    gains = jnp.concatenate([gain] * stations, axis=0)
    return gains / jnp.sqrt(smooth + epsilon)


def cross_kernel(*refs, stations, windows, bands, rows, own):
    left = refs[:bands]
    if own:
        right, refs = left, refs[bands:]
        gain, window, out, scale_left, board = refs
        scale_right = scale_left
        scale_left[...] = block_scales(left, gain[...], window[...], stations, windows, rows)
    else:
        right, refs = refs[bands : 2 * bands], refs[2 * bands :]
        scale_left, gain, window, out, scale_right, board = refs
        scale_right[...] = block_scales(right, gain[...], window[...], stations, windows, rows)
    share = 1.0 / (bands * windows)
    step = min(16, rows)
    steps = rows // step

    def body(turn, carry):
        i = turn // steps
        q = pl.multiple_of(turn % steps * step, step)

        def cell(chunk, s, w, e):
            at = ((s * windows + w) * 2 + e) * rows + q
            return chunk[pl.ds(pl.multiple_of(at, step), step), :].astype(jnp.float32)

        real = [jnp.zeros((step, ROOT), jnp.float32) for _ in range(stations)]
        imag = [jnp.zeros((step, ROOT), jnp.float32) for _ in range(stations)]
        for k in range(bands):
            for w in range(windows):
                a, b = cell(left[k], i, w, 0), cell(left[k], i, w, 1)
                for j in range(stations):
                    c, d = cell(right[k], j, w, 0), cell(right[k], j, w, 1)
                    real[j] = real[j] + (a * c + b * d)
                    imag[j] = imag[j] + (b * c - a * d)
        here = scale_left[pl.ds(pl.multiple_of(i * rows + q, step), step), :] * share
        for j in range(stations):
            both = here * scale_right[pl.ds(pl.multiple_of(j * rows + q, step), step), :]
            to = pl.ds(q * stations + j, step, stride=stations)
            board[0, i, to, :] = real[j] * both
            board[1, i, to, :] = imag[j] * both
        return carry

    lax.fori_loop(0, stations * steps, body, 0)
    out[...] = board[...].astype(jnp.bfloat16)


def cross(left, right, scale, gain, stations, windows):
    bands = len(left)
    rows = gain.shape[0]
    own = right is None
    vmem = pl.BlockSpec(memory_space=pltpu.VMEM)
    shape = (2, stations, rows * stations, ROOT)
    scales = (stations * rows, ROOT)
    args = (*left, gain, smoother()) if own else (*left, *right, scale, gain, smoother())
    outs = [jax.ShapeDtypeStruct(shape, jnp.bfloat16)]
    scratch = [pltpu.VMEM(shape, jnp.float32)]
    if own:
        outs.append(jax.ShapeDtypeStruct(scales, jnp.float32))
    else:
        scratch.insert(0, pltpu.VMEM(scales, jnp.float32))
    result = pl.pallas_call(
        functools.partial(
            cross_kernel, stations=stations, windows=windows, bands=bands, rows=rows, own=own
        ),
        out_shape=outs,
        in_specs=[vmem] * len(args),
        out_specs=[vmem] * len(outs),
        scratch_shapes=scratch,
        name="own_cross" if own else "pair_cross",
    )(*args)
    spread = result[0].reshape(2, stations, rows, stations, ROOT).transpose(0, 1, 3, 2, 4)
    spread = spread.reshape(2, stations, stations, rows * ROOT)
    return (spread, result[1]) if own else spread


def brought(block, axis, distance):
    count = lax.axis_size(axis)
    return lax.ppermute(block, axis, [((i + distance) % count, i) for i in range(count)])


def local(traces, live_flag, response):
    stations, windows, _ = traces.shape
    bands = lax.axis_size("band")
    offset = lax.axis_size("sta") // 8
    sent = transform(traces, live_flag, bands)
    mine = [sent[0]] + [brought(sent[k], "band", -k) for k in range(1, bands)]
    near = [brought(chunk, "sta", offset) for chunk in mine]
    far = [brought(chunk, "sta", 2 * offset) for chunk in mine]
    gain = response.reshape(-1, ROOT)
    own_cross, scale = cross(mine, None, None, gain, stations, windows)
    far_cross = cross(mine, far, scale, gain, stations, windows)
    near_cross = cross(mine, near, scale, gain, stations, windows)
    return own_cross, near_cross, far_cross


def solution(mesh):
    in_specs = (P("sta", "band", None), P("sta", None), P("band"))
    out_specs = (P(None, "sta", None, "band"),) * 3
    return jax.shard_map(local, mesh=mesh, in_specs=in_specs, out_specs=out_specs, check_vma=False)
```

```python
import functools
import math

import jax
import jax.numpy as jnp
import numpy as np
from jax import lax
from jax.experimental import pallas as pl
from jax.experimental.pallas import tpu as pltpu
from jax.sharding import PartitionSpec as P

ROOT = 128
SMOOTH = 64
epsilon = 1e-06


@functools.cache
def tables():
    n = np.arange(ROOT)
    angle = 2.0 * math.pi * ((n[:, None] * n[None, :]) % ROOT) / ROOT
    first = np.concatenate([np.cos(angle), -np.sin(angle)], axis=1)
    twist = 2.0 * math.pi * (n[:, None] * n[None, :]) / (ROOT * ROOT)
    half = angle[:, : ROOT // 2]
    c, s = np.cos(half), np.sin(half)
    second = np.concatenate(
        [np.concatenate([c, -s], axis=1), np.concatenate([s, c], axis=1)], axis=0
    )
    return (
        jnp.asarray(first.T, jnp.bfloat16),
        jnp.asarray(np.cos(twist), jnp.float32),
        jnp.asarray(np.sin(twist), jnp.float32),
        jnp.asarray(second.T, jnp.bfloat16),
    )


@functools.cache
def smoother():
    src = np.arange(3 * ROOT)[:, None] - ROOT
    dst = np.arange(ROOT)[None, :]
    return jnp.asarray(np.abs(src - dst) <= SMOOTH, jnp.bfloat16)


def transform_kernel(
    band_ref, flag_ref, x_ref, first_ref, cos_ref, sin_ref, second_ref, *refs,
    stations, windows, bands,
):
    outs, (wide, full, edges) = refs[:bands], refs[bands:]
    rows = ROOT // 2 // bands
    here = band_ref[0]
    lane = lax.broadcasted_iota(jnp.int32, (1, ROOT), 1)
    for s in range(stations):
        wide[...] = x_ref[s].astype(jnp.float32)
        folded = jnp.concatenate(
            [
                wide[pl.ds(w, ROOT, stride=windows), :].astype(jnp.bfloat16)
                for w in range(windows)
            ],
            axis=1,
        )
        one = jnp.dot(first_ref[...], folded, preferred_element_type=jnp.float32)
        for w in range(windows):
            real = one[:ROOT, w * ROOT : (w + 1) * ROOT]
            imag = one[ROOT:, w * ROOT : (w + 1) * ROOT]
            turned = jnp.concatenate(
                [
                    real * cos_ref[...] + imag * sin_ref[...],
                    imag * cos_ref[...] - real * sin_ref[...],
                ],
                axis=1,
            ).astype(jnp.bfloat16)
            two = lax.dot_general(
                second_ref[...], turned, (((1,), (1,)), ((), ())),
                preferred_element_type=jnp.float32,
            )
            gate = flag_ref[s, here * windows + w].astype(jnp.float32)
            full[...] = two * gate
            at = s * windows + w
            for k in range(bands):
                band = lax.rem(here + k, bands)
                start = pl.multiple_of(band * rows, 8)
                halves = []
                for e in range(2):
                    base = e * (ROOT // 2)
                    halves.append(full[pl.ds(base + start, rows), :])
                    after = full[pl.ds(base + jnp.minimum(start + rows, ROOT // 2 - 1), 1), :]
                    before = full[pl.ds(base + jnp.maximum(start - 1, 0), 1), :]
                    after = jnp.where(band == bands - 1, 0.0, after)
                    before = jnp.where(band == 0, 0.0, before)
                    edges[k, pl.ds(2 * at + e, 1), :] = jnp.where(lane < SMOOTH, after, before)
                outs[k][pl.ds(2 * at * rows, 2 * rows), :] = jnp.concatenate(
                    halves, axis=0
                ).astype(jnp.bfloat16)
    body = 2 * stations * windows * rows
    for k in range(bands):
        outs[k][pl.ds(body, 2 * stations * windows), :] = edges[k].astype(jnp.bfloat16)


def transform(traces, live_flag, bands):
    stations, windows, samples = traces.shape
    packed = traces.reshape(stations, windows, ROOT, ROOT).transpose(0, 2, 1, 3)
    packed = packed.reshape(stations, ROOT * windows, ROOT)
    rows = ROOT // 2 // bands
    height = 2 * stations * windows * (rows + 1)
    band = lax.axis_index("band").astype(jnp.int32).reshape(1)
    smem = pl.BlockSpec(memory_space=pltpu.SMEM)
    vmem = pl.BlockSpec(memory_space=pltpu.VMEM)
    return pl.pallas_call(
        functools.partial(transform_kernel, stations=stations, windows=windows, bands=bands),
        out_shape=[pltpu.VMEM((height, ROOT), jnp.bfloat16)] * bands,
        in_specs=[smem, smem] + [vmem] * 5,
        out_specs=[vmem] * bands,
        scratch_shapes=[
            pltpu.VMEM((ROOT * windows, ROOT), jnp.float32),
            pltpu.VMEM((ROOT, ROOT), jnp.float32),
            pltpu.VMEM((bands, 2 * stations * windows, ROOT), jnp.float32),
        ],
        name="transform",
    )(band, live_flag, packed, *tables())


def block_scales(chunks, gain, window, stations, windows, rows):
    body = 2 * stations * windows * rows
    total = len(chunks) * windows
    parts = []
    for s in range(stations):
        power = jnp.zeros((rows, ROOT), jnp.float32)
        edge = jnp.zeros((1, ROOT), jnp.float32)
        for chunk in chunks:
            for w in range(windows):
                at = 2 * (s * windows + w)
                cell = chunk[pl.ds(at * rows, 2 * rows), :].astype(jnp.float32)
                power = power + cell[:rows] * cell[:rows] + cell[rows:] * cell[rows:]
        parts.append(power)
    edges = []
    for chunk in chunks:
        line = chunk[pl.ds(body, 2 * stations * windows), :].astype(jnp.float32)
        edges.append(line * line)
    edges = sum(edges[1:], edges[0])
    rows_of = []
    for s in range(stations):
        span = 2 * windows
        edge = jnp.sum(edges[s * span : (s + 1) * span], axis=0, keepdims=True)
        power = parts[s]
        before = jnp.concatenate([edge, power[:-1]], axis=0)
        after = jnp.concatenate([power[1:], edge], axis=0)
        rows_of.append(jnp.concatenate([before, power, after], axis=1))
    spread = jnp.concatenate(rows_of, axis=0)
    high = spread.astype(jnp.bfloat16)
    rest = spread - high.astype(jnp.float32)
    middle = rest.astype(jnp.bfloat16)
    low = (rest - middle.astype(jnp.float32)).astype(jnp.bfloat16)
    smooth = sum(
        jnp.dot(part, window, preferred_element_type=jnp.float32) for part in (low, middle, high)
    ) / ((2 * SMOOTH + 1) * total)
    gains = jnp.concatenate([gain] * stations, axis=0)
    return gains / jnp.sqrt(smooth + epsilon)


def cross_kernel(*refs, stations, windows, bands, rows, own):
    left = refs[:bands]
    if own:
        right, refs = left, refs[bands:]
        gain, window, out, scale_left, board = refs
        scale_right = scale_left
        scale_left[...] = block_scales(left, gain[...], window[...], stations, windows, rows)
    else:
        right, refs = refs[bands : 2 * bands], refs[2 * bands :]
        scale_left, gain, window, out, scale_right, board = refs
        scale_right[...] = block_scales(right, gain[...], window[...], stations, windows, rows)
    share = 1.0 / (bands * windows)
    step = min(16, rows)
    steps = rows // step

    def body(turn, carry):
        i = turn // steps
        q = pl.multiple_of(turn % steps * step, step)

        def cell(chunk, s, w, e):
            at = ((s * windows + w) * 2 + e) * rows + q
            return chunk[pl.ds(pl.multiple_of(at, step), step), :].astype(jnp.float32)

        real = [jnp.zeros((step, ROOT), jnp.float32) for _ in range(stations)]
        imag = [jnp.zeros((step, ROOT), jnp.float32) for _ in range(stations)]
        for k in range(bands):
            for w in range(windows):
                a, b = cell(left[k], i, w, 0), cell(left[k], i, w, 1)
                for j in range(stations):
                    c, d = cell(right[k], j, w, 0), cell(right[k], j, w, 1)
                    real[j] = real[j] + (a * c + b * d)
                    imag[j] = imag[j] + (b * c - a * d)
        here = scale_left[pl.ds(pl.multiple_of(i * rows + q, step), step), :] * share
        for j in range(stations):
            both = here * scale_right[pl.ds(pl.multiple_of(j * rows + q, step), step), :]
            to = pl.ds(q * stations + j, step, stride=stations)
            board[0, i, to, :] = real[j] * both
            board[1, i, to, :] = imag[j] * both
        return carry

    lax.fori_loop(0, stations * steps, body, 0)
    out[...] = board[...].astype(jnp.bfloat16)


def cross(left, right, scale, gain, stations, windows):
    bands = len(left)
    rows = gain.shape[0]
    own = right is None
    vmem = pl.BlockSpec(memory_space=pltpu.VMEM)
    shape = (2, stations, rows * stations, ROOT)
    scales = (stations * rows, ROOT)
    held = [pltpu.with_memory_space_constraint(c, pltpu.VMEM) for c in (*left, *(right or ()))]
    args = (*held, gain, smoother()) if own else (*held, scale, gain, smoother())
    outs = [jax.ShapeDtypeStruct(shape, jnp.bfloat16)]
    scratch = [pltpu.VMEM(shape, jnp.float32)]
    if own:
        outs.append(jax.ShapeDtypeStruct(scales, jnp.float32))
    else:
        scratch.insert(0, pltpu.VMEM(scales, jnp.float32))
    result = pl.pallas_call(
        functools.partial(
            cross_kernel, stations=stations, windows=windows, bands=bands, rows=rows, own=own
        ),
        out_shape=outs,
        in_specs=[vmem] * len(args),
        out_specs=[vmem] * len(outs),
        scratch_shapes=scratch,
        name="own_cross" if own else "pair_cross",
    )(*args)
    spread = result[0].reshape(2, stations, rows, stations, ROOT).transpose(0, 1, 3, 2, 4)
    spread = spread.reshape(2, stations, stations, rows * ROOT)
    return (spread, result[1]) if own else spread


def brought(block, axis, distance):
    count = lax.axis_size(axis)
    return lax.ppermute(block, axis, [((i + distance) % count, i) for i in range(count)])


def local(traces, live_flag, response):
    stations, windows, _ = traces.shape
    bands = lax.axis_size("band")
    offset = lax.axis_size("sta") // 8
    sent = transform(traces, live_flag, bands)
    mine = [sent[0]] + [brought(sent[k], "band", -k) for k in range(1, bands)]
    near = [brought(chunk, "sta", offset) for chunk in mine]
    far = [brought(chunk, "sta", 2 * offset) for chunk in mine]
    gain = response.reshape(-1, ROOT)
    own_cross, scale = cross(mine, None, None, gain, stations, windows)
    far_cross = cross(mine, far, scale, gain, stations, windows)
    near_cross = cross(mine, near, scale, gain, stations, windows)
    return own_cross, near_cross, far_cross


def solution(mesh):
    in_specs = (P("sta", "band", None), P("sta", None), P("band"))
    out_specs = (P(None, "sta", None, "band"),) * 3
    return jax.shard_map(local, mesh=mesh, in_specs=in_specs, out_specs=out_specs, check_vma=False)
```

```python
import functools
import math

import jax
import jax.numpy as jnp
import numpy as np
from jax import lax
from jax.experimental import pallas as pl
from jax.experimental.pallas import tpu as pltpu
from jax.sharding import PartitionSpec as P

ROOT = 128
SMOOTH = 64
epsilon = 1e-06


@functools.cache
def tables():
    n = np.arange(ROOT)
    angle = 2.0 * math.pi * ((n[:, None] * n[None, :]) % ROOT) / ROOT
    first = np.concatenate([np.cos(angle), -np.sin(angle)], axis=1)
    twist = 2.0 * math.pi * (n[:, None] * n[None, :]) / (ROOT * ROOT)
    half = angle[:, : ROOT // 2]
    c, s = np.cos(half), np.sin(half)
    second = np.concatenate(
        [np.concatenate([c, -s], axis=1), np.concatenate([s, c], axis=1)], axis=0
    )
    return (
        jnp.asarray(first.T, jnp.bfloat16),
        jnp.asarray(np.cos(twist), jnp.float32),
        jnp.asarray(np.sin(twist), jnp.float32),
        jnp.asarray(second.T, jnp.bfloat16),
    )


@functools.cache
def smoother():
    src = np.arange(3 * ROOT)[:, None] - ROOT
    dst = np.arange(ROOT)[None, :]
    return jnp.asarray(np.abs(src - dst) <= SMOOTH, jnp.bfloat16)


def transform_kernel(
    band_ref, flag_ref, x_ref, first_ref, cos_ref, sin_ref, second_ref, *refs, stations, windows, bands,
):
    outs, (wide, edges) = refs[:bands], refs[bands:]
    half = ROOT // 2
    rows = half // bands
    lane = lax.broadcasted_iota(jnp.int32, (1, ROOT), 1)
    none = jnp.zeros((1, ROOT), jnp.float32)
    for s in range(stations):
        wide[...] = x_ref[s].astype(jnp.float32)
        folded = jnp.concatenate(
            [
                wide[pl.ds(w, ROOT, stride=windows), :].astype(jnp.bfloat16)
                for w in range(windows)
            ],
            axis=1,
        )
        one = jnp.dot(first_ref[...], folded, preferred_element_type=jnp.float32)
        for w in range(windows):
            real = one[:ROOT, w * ROOT : (w + 1) * ROOT]
            imag = one[ROOT:, w * ROOT : (w + 1) * ROOT]
            turned = jnp.concatenate(
                [
                    real * cos_ref[...] + imag * sin_ref[...],
                    imag * cos_ref[...] - real * sin_ref[...],
                ],
                axis=1,
            ).astype(jnp.bfloat16)
            two = lax.dot_general(
                second_ref[...], turned, (((1,), (1,)), ((), ())),
                preferred_element_type=jnp.float32,
            ) * flag_ref[s, band_ref[0] * windows + w].astype(jnp.float32)
            at = s * windows + w
            for k in range(bands):
                low, high = k * rows, (k + 1) * rows
                for e in range(2):
                    part = two[e * half : (e + 1) * half]
                    after = part[high : high + 1] if high < half else none
                    before = part[low - 1 : low] if low else none
                    edges[k, pl.ds(2 * at + e, 1), :] = jnp.where(lane < SMOOTH, after, before)
                both = jnp.concatenate([two[low:high], two[half + low : half + high]], axis=0)
                outs[k][pl.ds(2 * at * rows, 2 * rows), :] = both.astype(jnp.bfloat16)
    body = 2 * stations * windows * rows
    for k in range(bands):
        outs[k][pl.ds(body, 2 * stations * windows), :] = edges[k].astype(jnp.bfloat16)


def transform(traces, live_flag, band, bands):
    stations, windows, samples = traces.shape
    packed = traces.reshape(stations, windows, ROOT, ROOT).transpose(0, 2, 1, 3)
    packed = packed.reshape(stations, ROOT * windows, ROOT)
    rows = ROOT // 2 // bands
    height = 2 * stations * windows * (rows + 1)
    smem = pl.BlockSpec(memory_space=pltpu.SMEM)
    vmem = pl.BlockSpec(memory_space=pltpu.VMEM)
    return pl.pallas_call(
        functools.partial(transform_kernel, stations=stations, windows=windows, bands=bands),
        out_shape=[pltpu.VMEM((height, ROOT), jnp.bfloat16)] * bands,
        in_specs=[smem, smem] + [vmem] * 5,
        out_specs=[vmem] * bands,
        scratch_shapes=[
            pltpu.VMEM((ROOT * windows, ROOT), jnp.float32),
            pltpu.VMEM((bands, 2 * stations * windows, ROOT), jnp.float32),
        ],
        name="transform",
    )(band.reshape(1), live_flag, packed, *tables())


def scales_of(power, edge, gain, window, stations, rows, total):
    spread = []
    for s in range(stations):
        own = power[s * rows : (s + 1) * rows]
        beside = edge[s : s + 1]
        before = jnp.concatenate([beside, own[:-1]], axis=0)
        after = jnp.concatenate([own[1:], beside], axis=0)
        spread.append(jnp.concatenate([before, own, after], axis=1))
    spread = jnp.concatenate(spread, axis=0)
    high = spread.astype(jnp.bfloat16)
    low = (spread - high.astype(jnp.float32)).astype(jnp.bfloat16)
    smooth = jnp.dot(low, window, preferred_element_type=jnp.float32)
    smooth = smooth + jnp.dot(high, window, preferred_element_type=jnp.float32)
    smooth = smooth * (1.0 / ((2 * SMOOTH + 1) * total))
    return jnp.concatenate([gain] * stations, axis=0) / jnp.sqrt(smooth + epsilon)


def cross_kernel(*refs, stations, windows, rows, chunks, total, own, first, last):
    refs = list(refs)

    def take(count):
        taken, refs[:] = refs[:count], refs[count:]
        return taken

    left = take(chunks)
    right = left if own else take(chunks)
    if not first:
        sums, power_in, edge_in = take(3)
    if last:
        gain, window = take(2)
        scale_left = None if own else take(1)[0]
        (out,) = take(1)
        scale_right, board = take(2)
        scale_left = scale_right if own else scale_left
    else:
        sums_out, power_out, edge_out = take(3)

    body = 2 * stations * windows * rows
    power, edge = [], []
    for s in range(stations):
        cells = []
        lines = []
        for chunk in right:
            for w in range(windows):
                at = 2 * (s * windows + w)
                cell = chunk[pl.ds(at * rows, 2 * rows), :].astype(jnp.float32)
                cell = cell * cell
                cells.append(cell[:rows] + cell[rows:])
            line = chunk[pl.ds(body + 2 * s * windows, 2 * windows), :].astype(jnp.float32)
            lines.append(jnp.sum(line * line, axis=0, keepdims=True))
        power.append(sum(cells[1:], cells[0]))
        edge.append(sum(lines[1:], lines[0]))
    power, edge = jnp.concatenate(power, axis=0), jnp.concatenate(edge, axis=0)
    if not first:
        power, edge = power + power_in[...], edge + edge_in[...]
    if last:
        scale_right[...] = scales_of(power, edge, gain[...], window[...], stations, rows, total)
    else:
        power_out[...], edge_out[...] = power, edge

    step = min(16, rows)
    steps = rows // step

    def turn(index, carry):
        i = index // steps
        q = pl.multiple_of(index % steps * step, step)
        real, imag = [None] * stations, [None] * stations

        def cell(chunk, s, w, e):
            at = ((s * windows + w) * 2 + e) * rows + q
            return chunk[pl.ds(pl.multiple_of(at, step), step), :]

        def tree(terms):
            while len(terms) > 1:
                terms = [x + y for x, y in zip(terms[::2], terms[1::2])] + (
                    terms[-1:] if len(terms) % 2 else []
                )
            return terms[0].astype(jnp.float32)

        for k in range(chunks):
            a = [cell(left[k], i, w, 0) for w in range(windows)]
            b = [cell(left[k], i, w, 1) for w in range(windows)]
            for j in range(stations):
                c = [cell(right[k], j, w, 0) for w in range(windows)]
                d = [cell(right[k], j, w, 1) for w in range(windows)]
                re = tree([a[w] * c[w] + b[w] * d[w] for w in range(windows)])
                im = tree([b[w] * c[w] - a[w] * d[w] for w in range(windows)])
                real[j] = re if k == 0 else real[j] + re
                imag[j] = im if k == 0 else imag[j] + im
        if last:
            here = scale_left[pl.ds(pl.multiple_of(i * rows + q, step), step), :] * (1.0 / total)
        for j in range(stations):
            to = pl.ds(q, step)
            if not first:
                real[j] = real[j] + sums[0, i, j, to, :]
                imag[j] = imag[j] + sums[1, i, j, to, :]
            if last:
                both = here * scale_right[pl.ds(pl.multiple_of(j * rows + q, step), step), :]
                to = pl.ds(q * stations + j, step, stride=stations)
                board[0, i, to, :] = real[j] * both
                board[1, i, to, :] = imag[j] * both
            else:
                sums_out[0, i, j, to, :] = real[j]
                sums_out[1, i, j, to, :] = imag[j]
        return carry

    lax.fori_loop(0, stations * steps, turn, 0)
    if last:
        out[...] = board[...].astype(jnp.bfloat16)


def cross(left, right, stations, windows, total, before=None, ends=None):
    own = right is None
    first, last = before is None, ends is not None
    chunks = len(left)
    rows = left[0].shape[0] // (2 * stations * windows) - 1
    vmem = pl.BlockSpec(memory_space=pltpu.VMEM)
    shape = (2, stations, rows * stations, ROOT)
    scales = (stations * rows, ROOT)
    args = [*left, *(right or ()), *(before or ())]
    args = [pltpu.with_memory_space_constraint(c, pltpu.VMEM) for c in args]
    if last:
        args += ends[:2]
        if not own:
            args.append(pltpu.with_memory_space_constraint(ends[2], pltpu.VMEM))
        outs = [jax.ShapeDtypeStruct(shape, jnp.bfloat16)]
        scratch = [pltpu.VMEM(shape, jnp.float32)]
        if own:
            outs.append(pltpu.VMEM(scales, jnp.float32))
        else:
            scratch.insert(0, pltpu.VMEM(scales, jnp.float32))
    else:
        outs = [
            pltpu.VMEM((2, stations, stations, rows, ROOT), jnp.float32),
            pltpu.VMEM(scales, jnp.float32),
            pltpu.VMEM((stations, ROOT), jnp.float32),
        ]
        scratch = []
    result = pl.pallas_call(
        functools.partial(
            cross_kernel, stations=stations, windows=windows, rows=rows, chunks=chunks,
            total=total, own=own, first=first, last=last,
        ),
        out_shape=outs,
        in_specs=[vmem] * len(args),
        out_specs=[vmem] * len(outs),
        scratch_shapes=scratch,
        name="own_cross" if own else "pair_cross" if last else "pair_sums",
    )(*args)
    if not last:
        return result
    spread = result[0].reshape(2, stations, rows, stations, ROOT).transpose(0, 1, 3, 2, 4)
    spread = spread.reshape(2, stations, stations, rows * ROOT)
    return (spread, result[1]) if own else spread


def brought(block, axis, distance):
    count = lax.axis_size(axis)
    return lax.ppermute(block, axis, [((i + distance) % count, i) for i in range(count)])


def local(traces, live_flag, response):
    stations, windows, _ = traces.shape
    bands = lax.axis_size("band")
    band = lax.axis_index("band").astype(jnp.int32)
    offset = lax.axis_size("sta") // 8
    total = live_flag.shape[1]
    split = transform(traces, live_flag, band, bands)
    sent = [
        lax.select_n((band + k) % bands, *split) if bands > 2
        else jnp.where(band == k, split[0], split[1])
        for k in range(bands)
    ] if bands > 1 else split
    mine = [sent[0]] + [brought(sent[k], "band", -k) for k in range(1, bands)]
    near = [brought(chunk, "sta", offset) for chunk in mine]
    far = [brought(chunk, "sta", 2 * offset) for chunk in mine]
    ends = [response.reshape(-1, ROOT), smoother()]
    own_cross, scale = cross(mine, None, stations, windows, total, ends=ends)
    ends.append(scale)

    def pair(theirs):
        if bands == 1:
            return cross(mine, theirs, stations, windows, total, ends=ends)
        sums = cross(mine[:1], theirs[:1], stations, windows, total)
        return cross(mine[1:], theirs[1:], stations, windows, total, before=sums, ends=ends)

    near_cross, far_cross = pair(near), pair(far)
    return own_cross, near_cross, far_cross


def solution(mesh):
    in_specs = (P("sta", "band", None), P("sta", None), P("band"))
    out_specs = (P(None, "sta", None, "band"),) * 3
    return jax.shard_map(local, mesh=mesh, in_specs=in_specs, out_specs=out_specs, check_vma=False)
```

```python
import functools
import math

import jax
import jax.numpy as jnp
import numpy as np
from jax import lax
from jax.experimental import pallas as pl
from jax.experimental.pallas import tpu as pltpu
from jax.sharding import PartitionSpec as P

ROOT = 128
SMOOTH = 64
epsilon = 1e-06


@functools.cache
def tables():
    n = np.arange(ROOT)
    angle = 2.0 * math.pi * ((n[:, None] * n[None, :]) % ROOT) / ROOT
    first = np.concatenate([np.cos(angle), -np.sin(angle)], axis=1)
    twist = 2.0 * math.pi * (n[:, None] * n[None, :]) / (ROOT * ROOT)
    half = angle[:, : ROOT // 2]
    c, s = np.cos(half), np.sin(half)
    second = np.concatenate(
        [np.concatenate([c, -s], axis=1), np.concatenate([s, c], axis=1)], axis=0
    )
    return (
        jnp.asarray(first.T, jnp.bfloat16),
        jnp.asarray(np.cos(twist), jnp.float32),
        jnp.asarray(np.sin(twist), jnp.float32),
        jnp.asarray(second.T, jnp.bfloat16),
    )


@functools.cache
def smoother():
    src = np.arange(3 * ROOT)[:, None] - ROOT
    dst = np.arange(ROOT)[None, :]
    return jnp.asarray(np.abs(src - dst) <= SMOOTH, jnp.bfloat16)


def parts_of(stations):
    return 2 if stations % 2 == 0 else 1


def transform_kernel(
    band_ref, flag_ref, x_ref, first_ref, cos_ref, sin_ref, second_ref, *refs, stations, windows, bands,
):
    parts = parts_of(stations)
    outs, (wide, edges) = refs[: bands * parts], refs[bands * parts :]
    per = stations // parts
    half = ROOT // 2
    rows = half // bands
    lane = lax.broadcasted_iota(jnp.int32, (1, ROOT), 1)
    none = jnp.zeros((1, ROOT), jnp.float32)
    for s in range(stations):
        wide[...] = x_ref[s].astype(jnp.float32)
        folded = jnp.concatenate(
            [
                wide[pl.ds(w, ROOT, stride=windows), :].astype(jnp.bfloat16)
                for w in range(windows)
            ],
            axis=1,
        )
        one = jnp.dot(first_ref[...], folded, preferred_element_type=jnp.float32)
        for w in range(windows):
            real = one[:ROOT, w * ROOT : (w + 1) * ROOT]
            imag = one[ROOT:, w * ROOT : (w + 1) * ROOT]
            turned = jnp.concatenate(
                [
                    real * cos_ref[...] + imag * sin_ref[...],
                    imag * cos_ref[...] - real * sin_ref[...],
                ],
                axis=1,
            ).astype(jnp.bfloat16)
            two = lax.dot_general(
                second_ref[...], turned, (((1,), (1,)), ((), ())),
                preferred_element_type=jnp.float32,
            ) * flag_ref[s, band_ref[0] * windows + w].astype(jnp.float32)
            at = s % per * windows + w
            for k in range(bands):
                piece = outs[k * parts + s // per]
                low, high = k * rows, (k + 1) * rows
                for e in range(2):
                    part = two[e * half : (e + 1) * half]
                    after = part[high : high + 1] if high < half else none
                    before = part[low - 1 : low] if low else none
                    edges[k, pl.ds(2 * (s * windows + w) + e, 1), :] = jnp.where(lane < SMOOTH, after, before)
                both = jnp.concatenate([two[low:high], two[half + low : half + high]], axis=0)
                piece[pl.ds(2 * at * rows, 2 * rows), :] = both.astype(jnp.bfloat16)
    lines = 2 * per * windows
    for k in range(bands):
        for h in range(parts):
            outs[k * parts + h][pl.ds(lines * rows, lines), :] = edges[
                k, h * lines : (h + 1) * lines
            ].astype(jnp.bfloat16)


def transform(traces, live_flag, band, bands):
    stations, windows, samples = traces.shape
    packed = traces.reshape(stations, windows, ROOT, ROOT).transpose(0, 2, 1, 3)
    packed = packed.reshape(stations, ROOT * windows, ROOT)
    rows = ROOT // 2 // bands
    parts = parts_of(stations)
    height = 2 * stations // parts * windows * (rows + 1)
    smem = pl.BlockSpec(memory_space=pltpu.SMEM)
    vmem = pl.BlockSpec(memory_space=pltpu.VMEM)
    pieces = pl.pallas_call(
        functools.partial(transform_kernel, stations=stations, windows=windows, bands=bands),
        out_shape=[pltpu.VMEM((height, ROOT), jnp.bfloat16)] * (bands * parts),
        in_specs=[smem, smem] + [vmem] * 5,
        out_specs=[vmem] * (bands * parts),
        scratch_shapes=[
            pltpu.VMEM((ROOT * windows, ROOT), jnp.float32),
            pltpu.VMEM((bands, 2 * stations * windows, ROOT), jnp.float32),
        ],
        name="transform",
    )(band.reshape(1), live_flag, packed, *tables())
    return [pieces[k * parts : (k + 1) * parts] for k in range(bands)]


def scales_of(power, edge, gain, window, stations, rows, total):
    spread = []
    for s in range(stations):
        own = power[s * rows : (s + 1) * rows]
        beside = edge[s : s + 1]
        before = jnp.concatenate([beside, own[:-1]], axis=0)
        after = jnp.concatenate([own[1:], beside], axis=0)
        spread.append(jnp.concatenate([before, own, after], axis=1))
    spread = jnp.concatenate(spread, axis=0)
    high = spread.astype(jnp.bfloat16)
    low = (spread - high.astype(jnp.float32)).astype(jnp.bfloat16)
    smooth = jnp.dot(low, window, preferred_element_type=jnp.float32)
    smooth = smooth + jnp.dot(high, window, preferred_element_type=jnp.float32)
    smooth = smooth * (1.0 / ((2 * SMOOTH + 1) * total))
    return jnp.concatenate([gain] * stations, axis=0) / jnp.sqrt(smooth + epsilon)


def cross_kernel(*refs, stations, windows, rows, chunks, total, own, first, last):
    refs = list(refs)
    parts = parts_of(stations)
    per = stations // parts

    def take(count):
        taken, refs[:] = refs[:count], refs[count:]
        return taken

    left = take(chunks * parts)
    right = left if own else take(chunks * parts)
    if not first:
        sums, power_in, edge_in = take(3)
    if last:
        gain, window = take(2)
        scale_left = None if own else take(1)[0]
        (out,) = take(1)
        scale_right, board, ready, sems = take(4)
        scale_left = scale_right if own else scale_left
    else:
        sums_out, power_out, edge_out = take(3)

    body = 2 * per * windows * rows
    power, edge = [], []
    for s in range(stations):
        cells = []
        lines = []
        for k in range(chunks):
            chunk = right[k * parts + s // per]
            for w in range(windows):
                at = 2 * (s % per * windows + w)
                cell = chunk[pl.ds(at * rows, 2 * rows), :].astype(jnp.float32)
                cell = cell * cell
                cells.append(cell[:rows] + cell[rows:])
            line = chunk[pl.ds(body + 2 * (s % per) * windows, 2 * windows), :]
            line = line.astype(jnp.float32)
            lines.append(jnp.sum(line * line, axis=0, keepdims=True))
        power.append(sum(cells[1:], cells[0]))
        edge.append(sum(lines[1:], lines[0]))
    power, edge = jnp.concatenate(power, axis=0), jnp.concatenate(edge, axis=0)
    if not first:
        power, edge = power + power_in[...], edge + edge_in[...]
    if last:
        scale_right[...] = scales_of(power, edge, gain[...], window[...], stations, rows, total)
    else:
        power_out[...], edge_out[...] = power, edge

    step = min(16, rows)
    steps = rows // step

    def stored(e, i):
        return pltpu.make_async_copy(ready.at[e, i], out.at[e, i], sems.at[e, i])

    def tree(terms):
        while len(terms) > 1:
            terms = [x + y for x, y in zip(terms[::2], terms[1::2])] + (
                terms[-1:] if len(terms) % 2 else []
            )
        return terms[0].astype(jnp.float32)

    for i in range(stations):

        def turn(index, carry, i=i):
            q = pl.multiple_of(index * step, step)
            real, imag = [None] * stations, [None] * stations

            def cell(pieces, k, s, w, e):
                at = ((s % per * windows + w) * 2 + e) * rows
                return pieces[k * parts + s // per][pl.ds(pl.multiple_of(at + q, step), step), :]

            for k in range(chunks):
                a = [cell(left, k, i, w, 0) for w in range(windows)]
                b = [cell(left, k, i, w, 1) for w in range(windows)]
                for j in range(stations):
                    c = [cell(right, k, j, w, 0) for w in range(windows)]
                    d = [cell(right, k, j, w, 1) for w in range(windows)]
                    re = tree([a[w] * c[w] + b[w] * d[w] for w in range(windows)])
                    im = tree([b[w] * c[w] - a[w] * d[w] for w in range(windows)])
                    real[j] = re if k == 0 else real[j] + re
                    imag[j] = im if k == 0 else imag[j] + im
            if last:
                here = scale_left[pl.ds(pl.multiple_of(i * rows + q, step), step), :]
                here = here * (1.0 / total)
            for j in range(stations):
                to = pl.ds(q, step)
                if not first:
                    real[j] = real[j] + sums[0, i, j, to, :]
                    imag[j] = imag[j] + sums[1, i, j, to, :]
                if last:
                    there = scale_right[pl.ds(pl.multiple_of(j * rows + q, step), step), :]
                    to = pl.ds(q * stations + j, step, stride=stations)
                    board[0, to, :] = real[j] * (here * there)
                    board[1, to, :] = imag[j] * (here * there)
                else:
                    sums_out[0, i, j, to, :] = real[j]
                    sums_out[1, i, j, to, :] = imag[j]
            return carry

        lax.fori_loop(0, steps, turn, 0)
        if last:
            ready[:, i] = board[...].astype(jnp.bfloat16)
            for e in range(2):
                stored(e, i).start()
    if last:
        for i in range(stations):
            for e in range(2):
                stored(e, i).wait()


def cross(left, right, stations, windows, total, before=None, ends=None):
    own = right is None
    first, last = before is None, ends is not None
    chunks, parts = len(left), parts_of(stations)
    rows = left[0][0].shape[0] // (2 * stations // parts * windows) - 1
    vmem = pl.BlockSpec(memory_space=pltpu.VMEM)
    shape = (2, stations, rows * stations, ROOT)
    scales = (stations * rows, ROOT)
    args = [piece for chunk in (*left, *(right or ())) for piece in chunk]
    args += [*(before or ()), *(ends or ())]
    args = [pltpu.with_memory_space_constraint(c, pltpu.VMEM) for c in args]
    if last:
        outs = [jax.ShapeDtypeStruct(shape, jnp.bfloat16)]
        out_specs = [pl.BlockSpec(memory_space=pl.ANY)]
        scratch = [
            pltpu.VMEM((2, *shape[2:]), jnp.float32),
            pltpu.VMEM(shape, jnp.bfloat16),
            pltpu.SemaphoreType.DMA((2, stations)),
        ]
        if own:
            outs.append(pltpu.VMEM(scales, jnp.float32))
            out_specs.append(vmem)
        else:
            scratch.insert(0, pltpu.VMEM(scales, jnp.float32))
    else:
        outs = [
            pltpu.VMEM((2, stations, stations, rows, ROOT), jnp.float32),
            pltpu.VMEM(scales, jnp.float32),
            pltpu.VMEM((stations, ROOT), jnp.float32),
        ]
        out_specs = [vmem] * 3
        scratch = []
    result = pl.pallas_call(
        functools.partial(
            cross_kernel, stations=stations, windows=windows, rows=rows, chunks=chunks,
            total=total, own=own, first=first, last=last,
        ),
        out_shape=outs,
        in_specs=[vmem] * len(args),
        out_specs=out_specs,
        scratch_shapes=scratch,
        name="own_cross" if own else "pair_cross" if last else "pair_sums",
    )(*args)
    if not last:
        return result
    spread = result[0].reshape(2, stations, rows, stations, ROOT).transpose(0, 1, 3, 2, 4)
    spread = spread.reshape(2, stations, stations, rows * ROOT)
    return (spread, result[1]) if own else spread


def brought(block, axis, distance):
    count = lax.axis_size(axis)
    return lax.ppermute(block, axis, [((i + distance) % count, i) for i in range(count)])


def local(traces, live_flag, response):
    stations, windows, _ = traces.shape
    bands, parts = lax.axis_size("band"), parts_of(stations)
    band = lax.axis_index("band").astype(jnp.int32)
    blocks = lax.axis_size("sta")
    offset = blocks // 8
    total = live_flag.shape[1]
    split = transform(traces, live_flag, band, bands)
    even = lax.rem(lax.div(lax.axis_index("sta"), offset), 2) == 0
    relay = [(i, i + offset if i // offset % 2 == 0 else i - offset) for i in range(blocks)]

    def sent(k, h):
        pieces = [split[b][h] for b in range(bands)]
        if bands == 2:
            return jnp.where(band == k, *pieces)
        return lax.select_n((band + k) % bands, *pieces) if bands > 1 else pieces[0]

    mine, far, near = [], [], []
    order = [(k, h) for k in range(bands) for h in range(parts)]
    for k, h in order:
        with jax.named_scope(f"band_{k}_{h}"):
            mine.append(brought(sent(k, h), "band", -k) if k else sent(k, h))
    for (k, h), piece in zip(order, mine):
        with jax.named_scope(f"far_{k}_{h}"):
            far.append(brought(piece, "sta", 2 * offset))
        with jax.named_scope(f"near_{k}_{h}"):
            if (k, h) == order[-1]:
                near.append(brought(piece, "sta", offset))
            else:
                near.append(lax.ppermute(jnp.where(even, far[-1], piece), "sta", relay))
    mine, far, near = (
        [pieces[k * parts : (k + 1) * parts] for k in range(bands)] for pieces in (mine, far, near)
    )
    ends = [response.reshape(-1, ROOT), smoother()]
    with jax.named_scope("own"):
        own_cross, scale = cross(mine, None, stations, windows, total, ends=ends)
    ends.append(scale)

    def pair(theirs):
        if bands == 1:
            return cross(mine, theirs, stations, windows, total, ends=ends)
        sums = cross(mine[:1], theirs[:1], stations, windows, total)
        return cross(mine[1:], theirs[1:], stations, windows, total, before=sums, ends=ends)

    with jax.named_scope("farcross"):
        far_cross = pair(far)
    with jax.named_scope("nearcross"):
        near_cross = pair(near)
    return own_cross, near_cross, far_cross


def solution(mesh):
    in_specs = (P("sta", "band", None), P("sta", None), P("band"))
    out_specs = (P(None, "sta", None, "band"),) * 3
    return jax.shard_map(local, mesh=mesh, in_specs=in_specs, out_specs=out_specs, check_vma=False)
```

```python
import functools
import math

import jax
import jax.numpy as jnp
import numpy as np
from jax import lax
from jax.experimental import pallas as pl
from jax.experimental.pallas import tpu as pltpu
from jax.sharding import PartitionSpec as P


ROOT = 128
SMOOTH = 64
epsilon = 1e-06

C_HALVES = True
X_HALVES = True
O_HALVES = True
DIAGONAL = ()
DIRECT = ("1_1",)


@functools.cache
def tables():
    n = np.arange(ROOT)
    angle = 2.0 * math.pi * ((n[:, None] * n[None, :]) % ROOT) / ROOT
    first = np.concatenate([np.cos(angle), -np.sin(angle)], axis=1)
    step = 2.0 * math.pi * n[None, :] / (ROOT * ROOT)
    coarse, fine = 8 * np.arange(ROOT // 8)[:, None] * step, np.arange(8)[:, None] * step
    turns = [np.cos(coarse), np.sin(coarse), np.cos(fine), np.sin(fine)]
    return (
        jnp.asarray(first.T, jnp.bfloat16),
        jnp.asarray(np.concatenate(turns, axis=0), jnp.float32),
    )


@functools.cache
def smoother():
    src = np.arange(3 * ROOT)[:, None] - ROOT
    dst = np.arange(ROOT)[None, :]
    return jnp.asarray(np.abs(src - dst) <= SMOOTH, jnp.bfloat16)


def parts_of(stations):
    return 2 if stations % 2 == 0 else 1


def transformed(x, gate, held, outs, wide, edges, stations, windows, bands):
    first, cosine, sine = held
    half = ROOT // 2
    rows = half // bands
    cos_part, sin_part = first[:half, :], first[ROOT : ROOT + half, :]
    second = jnp.concatenate(
        [
            jnp.concatenate([cos_part, -sin_part], axis=1),
            jnp.concatenate([sin_part, cos_part], axis=1),
        ],
        axis=0,
    )
    lane = lax.broadcasted_iota(jnp.int32, (1, ROOT), 1)
    none = jnp.zeros((1, ROOT), jnp.float32)
    for s in range(stations):
        wide[...] = x(s).astype(jnp.float32)
        folded = jnp.concatenate(
            [
                wide[pl.ds(w, ROOT, stride=windows), :].astype(jnp.bfloat16)
                for w in range(windows)
            ],
            axis=1,
        )
        one = jnp.dot(first[...], folded, preferred_element_type=jnp.float32)
        for w in range(windows):
            real = one[:ROOT, w * ROOT : (w + 1) * ROOT]
            imag = one[ROOT:, w * ROOT : (w + 1) * ROOT]
            turned = jnp.concatenate(
                [
                    real * cosine[...] + imag * sine[...],
                    imag * cosine[...] - real * sine[...],
                ],
                axis=1,
            ).astype(jnp.bfloat16)
            at = s * windows + w
            two = lax.dot_general(
                second, turned, (((1,), (1,)), ((), ())),
                preferred_element_type=jnp.float32,
            ) * gate(at)
            for k in range(bands):
                low, high = k * rows, (k + 1) * rows
                for e in range(2):
                    part = two[e * half : (e + 1) * half]
                    after = part[high : high + 1] if high < half else none
                    before = part[low - 1 : low] if low else none
                    edges[k, pl.ds(2 * at + e, 1), :] = jnp.where(lane < SMOOTH, after, before)
                both = jnp.concatenate([two[low:high], two[half + low : half + high]], axis=0)
                outs[k][pl.ds(2 * at * rows, 2 * rows), :] = both.astype(jnp.bfloat16)
    lines = 2 * stations * windows
    for k in range(bands):
        outs[k][pl.ds(lines * rows, lines), :] = edges[k].astype(jnp.bfloat16)


def first_half_kernel(given_flags, x_ref, given, given_turns, *refs, stations, windows, bands):
    parts = parts_of(stations)
    per = stations // parts
    outs, held, refs = refs[:bands], refs[bands : bands + 3], refs[bands + 3 :]
    if parts > 1:
        later, gates, *refs = refs
    now, turns, wide, edges, flag_ref, sems = refs
    here = lax.axis_index("band").astype(jnp.int32)
    load_flags = pltpu.make_async_copy(given_flags, flag_ref, sems.at[3 + per])
    load_turns = pltpu.make_async_copy(given_turns, turns, sems.at[0])
    load_first = pltpu.make_async_copy(given, held[0], sems.at[1])
    arrivals = [
        pltpu.make_async_copy(x_ref.at[s], now.at[s], sems.at[2 + s]) for s in range(per)
    ]
    for load in (load_flags, load_turns, load_first, *arrivals):
        load.start()
    if parts > 1:
        rest = pltpu.make_async_copy(x_ref.at[pl.ds(per, per)], later, sems.at[2 + per])
        rest.start()

    def flag(at):
        return flag_ref[at // windows, here * windows + at % windows].astype(jnp.float32)

    load_flags.wait()
    if parts > 1:
        for at in range(per * windows):
            gates[pl.ds(at, 1), :] = jnp.full((1, ROOT), flag(per * windows + at), jnp.float32)
    load_turns.wait()
    count = ROOT // 8
    fine_cos, fine_sin = turns[2 * count : 2 * count + 8, :], turns[2 * count + 8 :, :]
    for i in range(count):
        cos, sin = turns[i : i + 1, :], turns[count + i : count + i + 1, :]
        held[1][pl.ds(8 * i, 8), :] = cos * fine_cos - sin * fine_sin
        held[2][pl.ds(8 * i, 8), :] = sin * fine_cos + cos * fine_sin
    load_first.wait()

    def x(s):
        arrivals[s].wait()
        return now[s]

    transformed(x, flag, held, outs, wide, edges, per, windows, bands)
    if parts > 1:
        rest.wait()


def second_half_kernel(x_ref, gates, *refs, stations, windows, bands):
    held, outs, (wide, edges) = refs[:3], refs[3 : 3 + bands], refs[3 + bands :]
    transformed(
        lambda s: x_ref[s], lambda at: gates[pl.ds(at, 1), :], held, outs, wide, edges,
        stations, windows, bands,
    )


def transform(traces, live_flag, bands):
    stations, windows, _ = traces.shape
    packed = traces.reshape(stations, windows, ROOT, ROOT).transpose(0, 2, 1, 3)
    packed = packed.reshape(stations, ROOT * windows, ROOT)
    rows = ROOT // 2 // bands
    parts = parts_of(stations)
    per = stations // parts
    height = 2 * per * windows * (rows + 1)
    vmem = pl.BlockSpec(memory_space=pltpu.VMEM)
    hbm = pl.BlockSpec(memory_space=pl.ANY)
    piece = pltpu.VMEM((height, ROOT), jnp.bfloat16)
    given = tables()
    shape = (per, ROOT * windows, ROOT)
    turned = pltpu.VMEM((ROOT, ROOT), jnp.float32)
    outs = [piece] * bands + [pltpu.VMEM(given[0].shape, jnp.bfloat16), turned, turned]
    if parts > 1:
        outs += [pltpu.VMEM(shape, jnp.bfloat16), pltpu.VMEM((per * windows, ROOT), jnp.float32)]
    scratch = [
        pltpu.VMEM((ROOT * windows, ROOT), jnp.float32),
        pltpu.VMEM((bands, 2 * per * windows, ROOT), jnp.float32),
    ]
    made = pl.pallas_call(
        functools.partial(first_half_kernel, stations=stations, windows=windows, bands=bands),
        out_shape=outs,
        in_specs=[hbm] * 4,
        out_specs=[vmem] * len(outs),
        scratch_shapes=[
            pltpu.VMEM(shape, jnp.bfloat16), pltpu.VMEM(given[1].shape, jnp.float32), *scratch,
            pltpu.SMEM(live_flag.shape, jnp.int32), pltpu.SemaphoreType.DMA((4 + per,)),
        ],
        name="transform_first",
    )(live_flag, packed, *given)
    halves = [made[:bands]]
    if parts > 1:
        held, later, gates = made[bands : bands + 3], made[bands + 3], made[bands + 4]
        args = [pltpu.with_memory_space_constraint(v, pltpu.VMEM) for v in (later, gates, *held)]
        halves.append(
            pl.pallas_call(
                functools.partial(second_half_kernel, stations=per, windows=windows, bands=bands),
                out_shape=[piece] * bands,
                in_specs=[vmem] * len(args),
                out_specs=[vmem] * bands,
                scratch_shapes=scratch,
                name="transform_second",
            )(*args)
        )
    return [[half[k] for half in halves] for k in range(bands)]


def scales_of(power, edge, gain, window, stations, rows, total):
    spread = []
    for s in range(stations):
        own = power[s * rows : (s + 1) * rows]
        beside = edge[s : s + 1]
        before = jnp.concatenate([beside, own[:-1]], axis=0)
        after = jnp.concatenate([own[1:], beside], axis=0)
        spread.append(jnp.concatenate([before, own, after], axis=1))
    spread = jnp.concatenate(spread, axis=0)
    high = spread.astype(jnp.bfloat16)
    low = (spread - high.astype(jnp.float32)).astype(jnp.bfloat16)
    smooth = jnp.dot(low, window, preferred_element_type=jnp.float32)
    smooth = smooth + jnp.dot(high, window, preferred_element_type=jnp.float32)
    smooth = smooth * (1.0 / ((2 * SMOOTH + 1) * total))
    return jnp.concatenate([gain] * stations, axis=0) / jnp.sqrt(smooth + epsilon)


def cross_kernel(*refs, stations, windows, rows, merges, theirs, total, own, first, last):
    refs = list(refs)
    chunks, parts = len(merges), parts_of(stations)
    per = stations // parts

    def take(count):
        taken, refs[:] = refs[:count], refs[count:]
        return taken

    def views(flags):
        pieces = []
        for merged in flags:
            if merged:
                height = 2 * per * windows * (rows + 1)
                (ref,) = take(1)
                pieces += [(ref, h * height) for h in range(parts)]
            else:
                pieces += [(ref, 0) for ref in take(parts)]
        return pieces

    left = views(merges)
    right = left if own else views(theirs)
    if not first:
        sums, power_in, edge_in = take(3)
    if last:
        gain, window = take(2)
        scale_left = None if own else take(1)[0]
        (out,) = take(1)
        scale_right, board, ready, sems = take(4)
        scale_left = scale_right if own else scale_left
    else:
        sums_out, power_out, edge_out = take(3)

    body = 2 * per * windows * rows
    power, edge = [], []
    for s in range(stations):
        cells = []
        lines = []
        for k in range(chunks):
            chunk, base = right[k * parts + s // per]
            for w in range(windows):
                at = 2 * (s % per * windows + w)
                cell = chunk[pl.ds(base + at * rows, 2 * rows), :].astype(jnp.float32)
                cell = cell * cell
                cells.append(cell[:rows] + cell[rows:])
            line = chunk[pl.ds(base + body + 2 * (s % per) * windows, 2 * windows), :]
            line = line.astype(jnp.float32)
            lines.append(jnp.sum(line * line, axis=0, keepdims=True))
        power.append(sum(cells[1:], cells[0]))
        edge.append(sum(lines[1:], lines[0]))
    power, edge = jnp.concatenate(power, axis=0), jnp.concatenate(edge, axis=0)
    if not first:
        power, edge = power + power_in[...], edge + edge_in[...]
    if last:
        scale_right[...] = scales_of(power, edge, gain[...], window[...], stations, rows, total)
    else:
        power_out[...], edge_out[...] = power, edge

    step = min(16, rows)
    steps = rows // step

    def stored(e, i):
        return pltpu.make_async_copy(ready.at[e, i], out.at[e, i], sems.at[e, i])

    def tree(terms):
        while len(terms) > 1:
            terms = [x + y for x, y in zip(terms[::2], terms[1::2])] + (
                terms[-1:] if len(terms) % 2 else []
            )
        return terms[0].astype(jnp.float32)

    for i in range(stations):

        def turn(index, carry, i=i):
            q = pl.multiple_of(index * step, step)
            real, imag = [None] * stations, [None] * stations

            def cell(pieces, k, s, w, e):
                ref, base = pieces[k * parts + s // per]
                at = base + ((s % per * windows + w) * 2 + e) * rows
                return ref[pl.ds(pl.multiple_of(at + q, step), step), :]

            for k in range(chunks):
                a = [cell(left, k, i, w, 0) for w in range(windows)]
                b = [cell(left, k, i, w, 1) for w in range(windows)]
                for j in range(stations):
                    c = [cell(right, k, j, w, 0) for w in range(windows)]
                    d = [cell(right, k, j, w, 1) for w in range(windows)]
                    re = tree([a[w] * c[w] + b[w] * d[w] for w in range(windows)])
                    im = tree([b[w] * c[w] - a[w] * d[w] for w in range(windows)])
                    real[j] = re if k == 0 else real[j] + re
                    imag[j] = im if k == 0 else imag[j] + im
            if last:
                here = scale_left[pl.ds(pl.multiple_of(i * rows + q, step), step), :]
                here = here * (1.0 / total)
            for j in range(stations):
                to = pl.ds(q, step)
                if not first:
                    real[j] = real[j] + sums[0, i, j, to, :]
                    imag[j] = imag[j] + sums[1, i, j, to, :]
                if last:
                    there = scale_right[pl.ds(pl.multiple_of(j * rows + q, step), step), :]
                    to = pl.ds(q * stations + j, step, stride=stations)
                    board[0, to, :] = real[j] * (here * there)
                    board[1, to, :] = imag[j] * (here * there)
                else:
                    sums_out[0, i, j, to, :] = real[j]
                    sums_out[1, i, j, to, :] = imag[j]
            return carry

        lax.fori_loop(0, steps, turn, 0)
        if last:
            ready[:, i] = board[...].astype(jnp.bfloat16)
            for e in range(2):
                stored(e, i).start()
    if last:
        for i in range(stations):
            for e in range(2):
                stored(e, i).wait()


def cross(left, right, stations, windows, total, before=None, ends=None):
    own = right is None
    first, last = before is None, ends is not None
    merges, theirs = (
        tuple(len(chunk) == 1 and parts_of(stations) > 1 for chunk in side)
        for side in (left, right or left)
    )
    height = sum(piece.shape[0] for piece in left[0])
    rows = height // (2 * stations * windows) - 1
    vmem = pl.BlockSpec(memory_space=pltpu.VMEM)
    shape = (2, stations, rows * stations, ROOT)
    scales = (stations * rows, ROOT)
    args = [piece for chunk in (*left, *(right or ())) for piece in chunk]
    args += [*(before or ()), *(ends or ())]
    args = [pltpu.with_memory_space_constraint(c, pltpu.VMEM) for c in args]
    if last:
        outs = [jax.ShapeDtypeStruct(shape, jnp.bfloat16)]
        out_specs = [pl.BlockSpec(memory_space=pl.ANY)]
        scratch = [
            pltpu.VMEM((2, *shape[2:]), jnp.float32),
            pltpu.VMEM(shape, jnp.bfloat16),
            pltpu.SemaphoreType.DMA((2, stations)),
        ]
        if own:
            outs.append(pltpu.VMEM(scales, jnp.float32))
            out_specs.append(vmem)
        else:
            scratch.insert(0, pltpu.VMEM(scales, jnp.float32))
    else:
        outs = [
            pltpu.VMEM((2, stations, stations, rows, ROOT), jnp.float32),
            pltpu.VMEM(scales, jnp.float32),
            pltpu.VMEM((stations, ROOT), jnp.float32),
        ]
        out_specs = [vmem] * 3
        scratch = []
    result = pl.pallas_call(
        functools.partial(
            cross_kernel, stations=stations, windows=windows, rows=rows, merges=merges,
            theirs=theirs,            total=total, own=own, first=first, last=last,
        ),
        out_shape=outs,
        in_specs=[vmem] * len(args),
        out_specs=out_specs,
        scratch_shapes=scratch,
        name="own_cross" if own else "pair_cross" if last else "pair_sums",
    )(*args)
    if not last:
        return result
    spread = result[0].reshape(2, stations, rows, stations, ROOT).transpose(0, 1, 3, 2, 4)
    spread = spread.reshape(2, stations, stations, rows * ROOT)
    return (spread, result[1]) if own else spread


def brought(block, axis, distance):
    count = lax.axis_size(axis)
    return lax.ppermute(block, axis, [((i + distance) % count, i) for i in range(count)])


def program(traces, live_flag, response):
    stations, windows, _ = traces.shape
    bands, parts = lax.axis_size("band"), parts_of(stations)
    band = lax.axis_index("band").astype(jnp.int32)
    blocks = lax.axis_size("sta")
    offset = blocks // 8
    total = live_flag.shape[1]
    split = transform(traces, live_flag, bands)
    even = lax.rem(lax.div(lax.axis_index("sta"), offset), 2) == 0
    relay = [(i, i + offset if i // offset % 2 == 0 else i - offset) for i in range(blocks)]

    def sent(k, h):
        pieces = [split[b][h] for b in range(bands)]
        if bands == 2:
            return jnp.where(band == k, *pieces)
        return lax.select_n((band + k) % bands, *pieces) if bands > 1 else pieces[0]

    def joined(k, hs):
        return jnp.concatenate([sent(k, h) for h in hs], axis=0) if hs[1:] else sent(k, hs[0])

    def groups(halves):
        return [(h,) for h in range(parts)] if halves else [tuple(range(parts))]

    def across(piece, distance, k):
        if not k:
            return brought(piece, "sta", distance)
        route = [
            ((s + distance) % blocks * bands + (b - k) % bands, s * bands + b)
            for s in range(blocks)
            for b in range(bands)
        ]
        return lax.ppermute(piece, ("sta", "band"), route)

    mine, far, near = ([[] for _ in range(bands)] for _ in range(3))
    for k in range(bands):
        for hs in groups(X_HALVES if k else C_HALVES):
            piece = joined(k, hs)
            mine[k].append(brought(piece, "band", -k) if k else piece)
    for k in range(bands):
        for at, hs in enumerate(groups(O_HALVES if k else C_HALVES)):
            tag = f"{min(k, 1)}_{hs[0]}"
            if k and tag not in DIAGONAL:
                piece = mine[k][at]
                far[k].append(brought(piece, "sta", 2 * offset))
            else:
                piece = joined(k, hs)
                far[k].append(across(piece, 2 * offset, k))
            if tag in DIRECT:
                near[k].append(across(joined(k, hs), offset, k) if tag in DIAGONAL else brought(piece, "sta", offset))
            else:
                held = mine[k]
                if len(held) > 1 or not O_HALVES or not k:
                    held = held[at]
                else:
                    size = held[0].shape[0] // parts
                    held = held[0][at * size : (at + 1) * size]
                near[k].append(lax.ppermute(jnp.where(even, far[k][-1], held), "sta", relay))
    ends = [response.reshape(-1, ROOT), smoother()]
    own_cross, scale = cross(mine, None, stations, windows, total, ends=ends)
    ends.append(scale)

    def pair(theirs):
        if bands == 1:
            return cross(mine, theirs, stations, windows, total, ends=ends)
        sums = cross(mine[:1], theirs[:1], stations, windows, total)
        return cross(mine[1:], theirs[1:], stations, windows, total, before=sums, ends=ends)

    far_cross = pair(far)
    near_cross = pair(near)
    return own_cross, near_cross, far_cross


def solution(mesh):
    in_specs = (P("sta", "band", None), P("sta", None), P("band"))
    out_specs = (P(None, "sta", None, "band"),) * 3
    return jax.shard_map(program, mesh=mesh, in_specs=in_specs, out_specs=out_specs, check_vma=False)
```

```python
import functools
import math

import jax
import jax.numpy as jnp
import numpy as np
from jax import lax
from jax.experimental import pallas as pl
from jax.experimental.pallas import tpu as pltpu
from jax.sharding import PartitionSpec as P


ROOT = 128
SMOOTH = 64
epsilon = 1e-06

CUT = 2
DIRECT = ("1_1",)


@functools.cache
def tables():
    n = np.arange(ROOT)
    angle = 2.0 * math.pi * ((n[:, None] * n[None, :]) % ROOT) / ROOT
    first = np.concatenate([np.cos(angle), -np.sin(angle)], axis=1)
    step = 2.0 * math.pi * n[None, :] / (ROOT * ROOT)
    coarse, fine = 8 * np.arange(ROOT // 8)[:, None] * step, np.arange(8)[:, None] * step
    turns = [np.cos(coarse), np.sin(coarse), np.cos(fine), np.sin(fine)]
    return (
        jnp.asarray(first.T, jnp.bfloat16),
        jnp.asarray(np.concatenate(turns, axis=0), jnp.float32),
    )


@functools.cache
def smoother():
    src = np.arange(3 * ROOT)[:, None] - ROOT
    dst = np.arange(ROOT)[None, :]
    return jnp.asarray(np.abs(src - dst) <= SMOOTH, jnp.bfloat16)


def pieces_of(stations):
    return ((0, CUT), (CUT, stations - CUT)) if stations > CUT else ((0, stations),)


def place_of(station, stations):
    for h, (start, count) in enumerate(pieces_of(stations)):
        if station < start + count:
            return h, station - start


def transformed(x, gate, held, outs, wide, edges, stations, windows, bands):
    first, cosine, sine = held
    half = ROOT // 2
    rows = half // bands
    cos_part, sin_part = first[:half, :], first[ROOT : ROOT + half, :]
    second = jnp.concatenate(
        [
            jnp.concatenate([cos_part, -sin_part], axis=1),
            jnp.concatenate([sin_part, cos_part], axis=1),
        ],
        axis=0,
    )
    lane = lax.broadcasted_iota(jnp.int32, (1, ROOT), 1)
    none = jnp.zeros((1, ROOT), jnp.float32)
    for s in range(stations):
        wide[s] = x(s).astype(jnp.float32)
        folded = jnp.concatenate(
            [
                wide[s, pl.ds(w, ROOT, stride=windows), :].astype(jnp.bfloat16)
                for w in range(windows)
            ],
            axis=1,
        )
        one = jnp.dot(first[...], folded, preferred_element_type=jnp.float32)
        turned = []
        for w in range(windows):
            real = one[:ROOT, w * ROOT : (w + 1) * ROOT]
            imag = one[ROOT:, w * ROOT : (w + 1) * ROOT]
            pair = [
                real * cosine[...] + imag * sine[...],
                imag * cosine[...] - real * sine[...],
            ]
            turned.append(jnp.concatenate(pair, axis=1).astype(jnp.bfloat16))
        every = lax.dot_general(
            second, jnp.concatenate(turned, axis=0), (((1,), (1,)), ((), ())),
            preferred_element_type=jnp.float32,
        )
        for w in range(windows):
            at = s * windows + w
            two = every[:, w * ROOT : (w + 1) * ROOT] * gate(at)
            for k in range(bands):
                low, high = k * rows, (k + 1) * rows
                for e in range(2):
                    part = two[e * half : (e + 1) * half]
                    after = part[high : high + 1] if high < half else none
                    before = part[low - 1 : low] if low else none
                    edges[k, pl.ds(2 * at + e, 1), :] = jnp.where(lane < SMOOTH, after, before)
                both = jnp.concatenate([two[low:high], two[half + low : half + high]], axis=0)
                outs[k][pl.ds(2 * at * rows, 2 * rows), :] = both.astype(jnp.bfloat16)
    lines = 2 * stations * windows
    for k in range(bands):
        outs[k][pl.ds(lines * rows, lines), :] = edges[k].astype(jnp.bfloat16)


def first_half_kernel(given_flags, x_ref, given, given_turns, *refs, stations, windows, bands):
    parts, per = len(pieces_of(stations)), pieces_of(stations)[0][1]
    outs, held, refs = refs[:bands], refs[bands : bands + 3], refs[bands + 3 :]
    if parts > 1:
        later, gates, *refs = refs
    now, turns, wide, edges, flag_ref, sems = refs
    here = lax.axis_index("band").astype(jnp.int32)
    load_flags = pltpu.make_async_copy(given_flags, flag_ref, sems.at[3 + per])
    load_turns = pltpu.make_async_copy(given_turns, turns, sems.at[0])
    load_first = pltpu.make_async_copy(given, held[0], sems.at[1])
    arrivals = [
        pltpu.make_async_copy(x_ref.at[s], now.at[s], sems.at[2 + s]) for s in range(per)
    ]
    for load in (arrivals[0], load_first, load_turns, load_flags, *arrivals[1:]):
        load.start()
    if parts > 1:
        rest = pltpu.make_async_copy(x_ref.at[pl.ds(per, stations - per)], later, sems.at[2 + per])
        rest.start()

    def flag(at):
        return flag_ref[at // windows, here * windows + at % windows].astype(jnp.float32)

    load_flags.wait()
    if parts > 1:
        for at in range((stations - per) * windows):
            gates[pl.ds(at, 1), :] = jnp.full((1, ROOT), flag(per * windows + at), jnp.float32)
    load_turns.wait()
    count = ROOT // 8
    fine_cos, fine_sin = turns[2 * count : 2 * count + 8, :], turns[2 * count + 8 :, :]
    for i in range(count):
        cos, sin = turns[i : i + 1, :], turns[count + i : count + i + 1, :]
        held[1][pl.ds(8 * i, 8), :] = cos * fine_cos - sin * fine_sin
        held[2][pl.ds(8 * i, 8), :] = sin * fine_cos + cos * fine_sin
    load_first.wait()

    def x(s):
        arrivals[s].wait()
        return now[s]

    transformed(x, flag, held, outs, wide, edges, per, windows, bands)
    if parts > 1:
        rest.wait()


def second_half_kernel(x_ref, gates, *refs, stations, windows, bands):
    held, outs, (wide, edges) = refs[:3], refs[3 : 3 + bands], refs[3 + bands :]
    transformed(
        lambda s: x_ref[s], lambda at: gates[pl.ds(at, 1), :], held, outs, wide, edges,
        stations, windows, bands,
    )


def transform(traces, live_flag, bands):
    stations, windows, _ = traces.shape
    packed = traces.reshape(stations, windows, ROOT, ROOT).transpose(0, 2, 1, 3)
    packed = packed.reshape(stations, ROOT * windows, ROOT)
    rows = ROOT // 2 // bands
    counts = [count for _, count in pieces_of(stations)]
    vmem = pl.BlockSpec(memory_space=pltpu.VMEM)
    hbm = pl.BlockSpec(memory_space=pl.ANY)
    given = tables()

    def outs_of(count):
        return [pltpu.VMEM((2 * count * windows * (rows + 1), ROOT), jnp.bfloat16)] * bands

    def block(count, dtype):
        return pltpu.VMEM((count, ROOT * windows, ROOT), dtype)

    def scratch_of(count):
        edges = pltpu.VMEM((bands, 2 * count * windows, ROOT), jnp.float32)
        return [block(count, jnp.float32), edges]

    turned = pltpu.VMEM((ROOT, ROOT), jnp.float32)
    outs = outs_of(counts[0]) + [pltpu.VMEM(given[0].shape, jnp.bfloat16), turned, turned]
    for count in counts[1:]:
        outs += [block(count, jnp.bfloat16), pltpu.VMEM((count * windows, ROOT), jnp.float32)]
    made = pl.pallas_call(
        functools.partial(first_half_kernel, stations=stations, windows=windows, bands=bands),
        out_shape=outs,
        in_specs=[hbm] * 4,
        out_specs=[vmem] * len(outs),
        scratch_shapes=[
            block(counts[0], jnp.bfloat16), pltpu.VMEM(given[1].shape, jnp.float32),
            *scratch_of(counts[0]), pltpu.SMEM(live_flag.shape, jnp.int32),
            pltpu.SemaphoreType.DMA((4 + counts[0],)),
        ],
        name="transform_first",
    )(live_flag, packed, *given)
    halves = [made[:bands]]
    for count in counts[1:]:
        held, (later, gates) = made[bands : bands + 3], made[bands + 3 :]
        args = [pltpu.with_memory_space_constraint(v, pltpu.VMEM) for v in (later, gates, *held)]
        halves.append(
            pl.pallas_call(
                functools.partial(second_half_kernel, stations=count, windows=windows, bands=bands),
                out_shape=outs_of(count),
                in_specs=[vmem] * len(args),
                out_specs=[vmem] * bands,
                scratch_shapes=scratch_of(count),
                name="transform_second",
            )(*args)
        )
    return [[half[k] for half in halves] for k in range(bands)]


def scales_of(power, edge, gain, window, stations, rows, total):
    spread = []
    for s in range(stations):
        own = power[s * rows : (s + 1) * rows]
        beside = edge[s : s + 1]
        before = jnp.concatenate([beside, own[:-1]], axis=0)
        after = jnp.concatenate([own[1:], beside], axis=0)
        spread.append(jnp.concatenate([before, own, after], axis=1))
    spread = jnp.concatenate(spread, axis=0)
    high = spread.astype(jnp.bfloat16)
    low = (spread - high.astype(jnp.float32)).astype(jnp.bfloat16)
    smooth = jnp.dot(low, window, preferred_element_type=jnp.float32)
    smooth = smooth + jnp.dot(high, window, preferred_element_type=jnp.float32)
    smooth = smooth * (1.0 / ((2 * SMOOTH + 1) * total))
    return jnp.concatenate([gain] * stations, axis=0) * lax.rsqrt(smooth + epsilon)


def cross_kernel(*refs, stations, windows, rows, chunks, total, own, first, last):
    refs = list(refs)
    parts = len(pieces_of(stations))

    def take(count):
        taken, refs[:] = refs[:count], refs[count:]
        return taken

    left = take(chunks * parts)
    right = left if own else take(chunks * parts)
    if not first:
        sums, power_in, edge_in = take(3)
    if last:
        gain, window = take(2)
        scale_left = None if own else take(1)[0]
        (out,) = take(1)
        scale_right, board, ready, sems = take(4)
        scale_left = scale_right if own else scale_left
    else:
        sums_out, power_out, edge_out = take(3)

    power, edge = [], []
    for s in range(stations):
        h, place = place_of(s, stations)
        body = 2 * pieces_of(stations)[h][1] * windows * rows
        cells = []
        lines = []
        for k in range(chunks):
            chunk = right[k * parts + h]
            for w in range(windows):
                at = 2 * (place * windows + w)
                cell = chunk[pl.ds(at * rows, 2 * rows), :].astype(jnp.float32)
                cell = cell * cell
                cells.append(cell[:rows] + cell[rows:])
            line = chunk[pl.ds(body + 2 * place * windows, 2 * windows), :]
            line = line.astype(jnp.float32)
            lines.append(jnp.sum(line * line, axis=0, keepdims=True))
        power.append(sum(cells[1:], cells[0]))
        edge.append(sum(lines[1:], lines[0]))
    power, edge = jnp.concatenate(power, axis=0), jnp.concatenate(edge, axis=0)
    if not first:
        power, edge = power + power_in[...], edge + edge_in[...]
    if last:
        scale_right[...] = scales_of(power, edge, gain[...], window[...], stations, rows, total)
    else:
        power_out[...], edge_out[...] = power, edge

    step = min(16, rows)
    steps = rows // step

    def stored(e, i):
        return pltpu.make_async_copy(ready.at[e, i], out.at[e, i], sems.at[e, i])

    def tree(terms):
        while len(terms) > 1:
            terms = [x + y for x, y in zip(terms[::2], terms[1::2])] + (
                terms[-1:] if len(terms) % 2 else []
            )
        return terms[0].astype(jnp.float32)

    for i in range(stations):

        def turn(index, carry, i=i):
            q = pl.multiple_of(index * step, step)
            real, imag = [None] * stations, [None] * stations

            def cell(pieces, k, s, w, e):
                h, place = place_of(s, stations)
                at = ((place * windows + w) * 2 + e) * rows
                return pieces[k * parts + h][pl.ds(pl.multiple_of(at + q, step), step), :]

            for k in range(chunks):
                a = [cell(left, k, i, w, 0) for w in range(windows)]
                b = [cell(left, k, i, w, 1) for w in range(windows)]
                for j in range(stations):
                    c = [cell(right, k, j, w, 0) for w in range(windows)]
                    d = [cell(right, k, j, w, 1) for w in range(windows)]
                    re = tree([a[w] * c[w] + b[w] * d[w] for w in range(windows)])
                    im = tree([b[w] * c[w] - a[w] * d[w] for w in range(windows)])
                    real[j] = re if k == 0 else real[j] + re
                    imag[j] = im if k == 0 else imag[j] + im
            if last:
                here = scale_left[pl.ds(pl.multiple_of(i * rows + q, step), step), :]
                here = here * (1.0 / total)
            for j in range(stations):
                to = pl.ds(q, step)
                if not first:
                    real[j] = real[j] + sums[0, i, j, to, :]
                    imag[j] = imag[j] + sums[1, i, j, to, :]
                if last:
                    there = scale_right[pl.ds(pl.multiple_of(j * rows + q, step), step), :]
                    to = pl.ds(q * stations + j, step, stride=stations)
                    board[0, to, :] = real[j] * (here * there)
                    board[1, to, :] = imag[j] * (here * there)
                else:
                    sums_out[0, i, j, to, :] = real[j]
                    sums_out[1, i, j, to, :] = imag[j]
            return carry

        lax.fori_loop(0, steps, turn, 0)
        if last:
            ready[:, i] = board[...].astype(jnp.bfloat16)
            for e in range(2):
                stored(e, i).start()
    if last:
        for i in range(stations):
            for e in range(2):
                stored(e, i).wait()


def cross(left, right, stations, windows, total, before=None, ends=None):
    own = right is None
    first, last = before is None, ends is not None
    chunks = len(left)
    height = sum(piece.shape[0] for piece in left[0])
    rows = height // (2 * stations * windows) - 1
    vmem = pl.BlockSpec(memory_space=pltpu.VMEM)
    shape = (2, stations, rows * stations, ROOT)
    scales = (stations * rows, ROOT)
    args = [piece for chunk in (*left, *(right or ())) for piece in chunk]
    args += [*(before or ()), *(ends or ())]
    args = [pltpu.with_memory_space_constraint(c, pltpu.VMEM) for c in args]
    if last:
        outs = [jax.ShapeDtypeStruct(shape, jnp.bfloat16)]
        out_specs = [pl.BlockSpec(memory_space=pl.ANY)]
        scratch = [
            pltpu.VMEM((2, *shape[2:]), jnp.float32),
            pltpu.VMEM(shape, jnp.bfloat16),
            pltpu.SemaphoreType.DMA((2, stations)),
        ]
        if own:
            outs.append(pltpu.VMEM(scales, jnp.float32))
            out_specs.append(vmem)
        else:
            scratch.insert(0, pltpu.VMEM(scales, jnp.float32))
    else:
        outs = [
            pltpu.VMEM((2, stations, stations, rows, ROOT), jnp.float32),
            pltpu.VMEM(scales, jnp.float32),
            pltpu.VMEM((stations, ROOT), jnp.float32),
        ]
        out_specs = [vmem] * 3
        scratch = []
    result = pl.pallas_call(
        functools.partial(
            cross_kernel, stations=stations, windows=windows, rows=rows, chunks=chunks,
            total=total, own=own, first=first, last=last,
        ),
        out_shape=outs,
        in_specs=[vmem] * len(args),
        out_specs=out_specs,
        scratch_shapes=scratch,
        name="own_cross" if own else "pair_cross" if last else "pair_sums",
    )(*args)
    if not last:
        return result
    spread = result[0].reshape(2, stations, rows, stations, ROOT).transpose(0, 1, 3, 2, 4)
    spread = spread.reshape(2, stations, stations, rows * ROOT)
    return (spread, result[1]) if own else spread


def brought(block, axis, distance):
    count = lax.axis_size(axis)
    return lax.ppermute(block, axis, [((i + distance) % count, i) for i in range(count)])


def program(traces, live_flag, response):
    stations, windows, _ = traces.shape
    bands, parts = lax.axis_size("band"), len(pieces_of(stations))
    band = lax.axis_index("band").astype(jnp.int32)
    blocks = lax.axis_size("sta")
    offset = blocks // 8
    total = live_flag.shape[1]
    split = transform(traces, live_flag, bands)
    even = lax.rem(lax.div(lax.axis_index("sta"), offset), 2) == 0
    relay = [(i, i + offset if i // offset % 2 == 0 else i - offset) for i in range(blocks)]

    def sent(k, h):
        pieces = [split[b][h] for b in range(bands)]
        if bands == 2:
            return jnp.where(band == k, *pieces)
        return lax.select_n((band + k) % bands, *pieces) if bands > 1 else pieces[0]

    mine, far, near = ([[] for _ in range(bands)] for _ in range(3))
    order = [(k, h, f"{min(k, 1)}_{h}") for k in range(bands) for h in range(parts)]
    for k, h, tag in order:
        mine[k].append(brought(sent(k, h), "band", -k) if k else sent(k, h))
    for k, h, tag in order:
        far[k].append(brought(mine[k][h], "sta", 2 * offset))
        if tag in DIRECT:
            near[k].append(brought(mine[k][h], "sta", offset))
        else:
            held = jnp.where(even, far[k][h], mine[k][h])
            near[k].append(lax.ppermute(held, "sta", relay))
    ends = [response.reshape(-1, ROOT), smoother()]
    own_cross, scale = cross(mine, None, stations, windows, total, ends=ends)
    ends.append(scale)

    def pair(theirs):
        if bands == 1:
            return cross(mine, theirs, stations, windows, total, ends=ends)
        sums = cross(mine[:1], theirs[:1], stations, windows, total)
        return cross(mine[1:], theirs[1:], stations, windows, total, before=sums, ends=ends)

    far_cross = pair(far)
    near_cross = pair(near)
    return own_cross, near_cross, far_cross


def solution(mesh):
    in_specs = (P("sta", "band", None), P("sta", None), P("band"))
    out_specs = (P(None, "sta", None, "band"),) * 3
    return jax.shard_map(program, mesh=mesh, in_specs=in_specs, out_specs=out_specs, check_vma=False)
```

```python
import functools
import math

import jax
import jax.numpy as jnp
import numpy as np
from jax import lax
from jax.experimental import pallas as pl
from jax.experimental.pallas import tpu as pltpu
from jax.sharding import PartitionSpec as P


ROOT = 128
SMOOTH = 64
epsilon = 1e-06

CUT = 2
DIRECT = ("1_1",)


@functools.cache
def tables():
    n = np.arange(ROOT)
    angle = 2.0 * math.pi * ((n[:, None] * n[None, :]) % ROOT) / ROOT
    first = np.concatenate([np.cos(angle), -np.sin(angle)], axis=1)
    step = 2.0 * math.pi * n[None, :] / (ROOT * ROOT)
    coarse, fine = 8 * np.arange(ROOT // 8)[:, None] * step, np.arange(8)[:, None] * step
    turns = [np.cos(coarse), np.sin(coarse), np.cos(fine), np.sin(fine)]
    return (
        jnp.asarray(first.T, jnp.bfloat16),
        jnp.asarray(np.concatenate(turns, axis=0), jnp.float32),
    )


@functools.cache
def smoother():
    src = np.arange(3 * ROOT)[:, None] - ROOT
    dst = np.arange(ROOT)[None, :]
    return jnp.asarray(np.abs(src - dst) <= SMOOTH, jnp.bfloat16)


def pieces_of(stations):
    return ((0, CUT), (CUT, stations - CUT)) if stations > CUT else ((0, stations),)


def place_of(station, stations):
    for h, (start, count) in enumerate(pieces_of(stations)):
        if station < start + count:
            return h, station - start


def transformed(x, gate, held, outs, wide, edges, stations, windows, bands):
    first, cosine, sine = held
    half = ROOT // 2
    rows = half // bands
    cos_part, sin_part = first[:half, :], first[ROOT : ROOT + half, :]
    second = jnp.concatenate(
        [
            jnp.concatenate([cos_part, -sin_part], axis=1),
            jnp.concatenate([sin_part, cos_part], axis=1),
        ],
        axis=0,
    )
    lane = lax.broadcasted_iota(jnp.int32, (1, ROOT), 1)
    none = jnp.zeros((1, ROOT), jnp.float32)
    for s in range(stations):
        wide[s] = x(s).astype(jnp.float32)
        folded = jnp.concatenate(
            [
                wide[s, pl.ds(w, ROOT, stride=windows), :].astype(jnp.bfloat16)
                for w in range(windows)
            ],
            axis=1,
        )
        one = jnp.dot(first[...], folded, preferred_element_type=jnp.float32)
        turned = []
        for w in range(windows):
            real = one[:ROOT, w * ROOT : (w + 1) * ROOT]
            imag = one[ROOT:, w * ROOT : (w + 1) * ROOT]
            pair = [
                real * cosine[...] + imag * sine[...],
                imag * cosine[...] - real * sine[...],
            ]
            turned.append(jnp.concatenate(pair, axis=1).astype(jnp.bfloat16))
        every = lax.dot_general(
            second, jnp.concatenate(turned, axis=0), (((1,), (1,)), ((), ())),
            preferred_element_type=jnp.float32,
        )
        for w in range(windows):
            at = s * windows + w
            two = every[:, w * ROOT : (w + 1) * ROOT] * gate(at)
            for k in range(bands):
                low, high = k * rows, (k + 1) * rows
                for e in range(2):
                    part = two[e * half : (e + 1) * half]
                    after = part[high : high + 1] if high < half else none
                    before = part[low - 1 : low] if low else none
                    edges[k, pl.ds(2 * at + e, 1), :] = jnp.where(lane < SMOOTH, after, before)
                both = jnp.concatenate([two[low:high], two[half + low : half + high]], axis=0)
                outs[k][pl.ds(2 * at * rows, 2 * rows), :] = both.astype(jnp.bfloat16)
    lines = 2 * stations * windows
    for k in range(bands):
        outs[k][pl.ds(lines * rows, lines), :] = edges[k].astype(jnp.bfloat16)


def first_half_kernel(given_flags, x_ref, given, given_turns, *refs, stations, windows, bands):
    parts, per = len(pieces_of(stations)), pieces_of(stations)[0][1]
    outs, held, refs = refs[:bands], refs[bands : bands + 3], refs[bands + 3 :]
    if parts > 1:
        later, gates, *refs = refs
    now, turns, wide, edges, flag_ref, sems = refs
    here = lax.axis_index("band").astype(jnp.int32)
    load_flags = pltpu.make_async_copy(given_flags, flag_ref, sems.at[3 + per])
    load_turns = pltpu.make_async_copy(given_turns, turns, sems.at[0])
    load_first = pltpu.make_async_copy(given, held[0], sems.at[1])
    arrivals = [
        pltpu.make_async_copy(x_ref.at[s], now.at[s], sems.at[2 + s]) for s in range(per)
    ]
    for load in (arrivals[0], load_first, load_turns, load_flags, *arrivals[1:]):
        load.start()
    if parts > 1:
        rest = pltpu.make_async_copy(x_ref.at[pl.ds(per, stations - per)], later, sems.at[2 + per])
        rest.start()

    def flag(at):
        return flag_ref[at // windows, here * windows + at % windows].astype(jnp.float32)

    load_flags.wait()
    if parts > 1:
        for at in range((stations - per) * windows):
            gates[pl.ds(at, 1), :] = jnp.full((1, ROOT), flag(per * windows + at), jnp.float32)
    load_turns.wait()
    count = ROOT // 8
    fine_cos, fine_sin = turns[2 * count : 2 * count + 8, :], turns[2 * count + 8 :, :]
    for i in range(count):
        cos, sin = turns[i : i + 1, :], turns[count + i : count + i + 1, :]
        held[1][pl.ds(8 * i, 8), :] = cos * fine_cos - sin * fine_sin
        held[2][pl.ds(8 * i, 8), :] = sin * fine_cos + cos * fine_sin
    load_first.wait()

    def x(s):
        arrivals[s].wait()
        return now[s]

    transformed(x, flag, held, outs, wide, edges, per, windows, bands)
    if parts > 1:
        rest.wait()


def second_half_kernel(x_ref, gates, *refs, stations, windows, bands):
    held, outs, (wide, edges) = refs[:3], refs[3 : 3 + bands], refs[3 + bands :]
    transformed(
        lambda s: x_ref[s], lambda at: gates[pl.ds(at, 1), :], held, outs, wide, edges,
        stations, windows, bands,
    )


def transform(traces, live_flag, bands):
    stations, windows, _ = traces.shape
    packed = traces.reshape(stations, windows, ROOT, ROOT).transpose(0, 2, 1, 3)
    packed = packed.reshape(stations, ROOT * windows, ROOT)
    rows = ROOT // 2 // bands
    counts = [count for _, count in pieces_of(stations)]
    vmem = pl.BlockSpec(memory_space=pltpu.VMEM)
    hbm = pl.BlockSpec(memory_space=pl.ANY)
    given = tables()

    def outs_of(count):
        return [pltpu.VMEM((2 * count * windows * (rows + 1), ROOT), jnp.bfloat16)] * bands

    def block(count, dtype):
        return pltpu.VMEM((count, ROOT * windows, ROOT), dtype)

    def scratch_of(count):
        edges = pltpu.VMEM((bands, 2 * count * windows, ROOT), jnp.float32)
        return [block(count, jnp.float32), edges]

    turned = pltpu.VMEM((ROOT, ROOT), jnp.float32)
    outs = outs_of(counts[0]) + [pltpu.VMEM(given[0].shape, jnp.bfloat16), turned, turned]
    for count in counts[1:]:
        outs += [block(count, jnp.bfloat16), pltpu.VMEM((count * windows, ROOT), jnp.float32)]
    made = pl.pallas_call(
        functools.partial(first_half_kernel, stations=stations, windows=windows, bands=bands),
        out_shape=outs,
        in_specs=[hbm] * 4,
        out_specs=[vmem] * len(outs),
        scratch_shapes=[
            block(counts[0], jnp.bfloat16), pltpu.VMEM(given[1].shape, jnp.float32),
            *scratch_of(counts[0]), pltpu.SMEM(live_flag.shape, jnp.int32),
            pltpu.SemaphoreType.DMA((4 + counts[0],)),
        ],
        name="transform_first",
    )(live_flag, packed, *given)
    halves = [made[:bands]]
    for count in counts[1:]:
        held, (later, gates) = made[bands : bands + 3], made[bands + 3 :]
        args = [pltpu.with_memory_space_constraint(v, pltpu.VMEM) for v in (later, gates, *held)]
        halves.append(
            pl.pallas_call(
                functools.partial(second_half_kernel, stations=count, windows=windows, bands=bands),
                out_shape=outs_of(count),
                in_specs=[vmem] * len(args),
                out_specs=[vmem] * bands,
                scratch_shapes=scratch_of(count),
                name="transform_second",
            )(*args)
        )
    return [[half[k] for half in halves] for k in range(bands)]


def scales_of(power, edge, gain, window, stations, rows, total):
    spread = []
    for s in range(stations):
        own = power[s * rows : (s + 1) * rows]
        beside = edge[s : s + 1]
        before = jnp.concatenate([beside, own[:-1]], axis=0)
        after = jnp.concatenate([own[1:], beside], axis=0)
        spread.append(jnp.concatenate([before, own, after], axis=1))
    spread = jnp.concatenate(spread, axis=0)
    high = spread.astype(jnp.bfloat16)
    low = (spread - high.astype(jnp.float32)).astype(jnp.bfloat16)
    smooth = jnp.dot(low, window, preferred_element_type=jnp.float32)
    smooth = smooth + jnp.dot(high, window, preferred_element_type=jnp.float32)
    smooth = smooth * (1.0 / ((2 * SMOOTH + 1) * total))
    return jnp.concatenate([gain] * stations, axis=0) * lax.rsqrt(smooth + epsilon)


def cross_kernel(*refs, stations, windows, rows, chunks, total, own, first, last):
    refs = list(refs)
    parts = len(pieces_of(stations))

    def take(count):
        taken, refs[:] = refs[:count], refs[count:]
        return taken

    left = take(chunks * parts)
    right = left if own else take(chunks * parts)
    if not first:
        sums, power_in, edge_in = take(3)
    if last:
        gain, window = take(2)
        scale_left = None if own else take(1)[0]
        (out,) = take(1)
        scale_right, board, ready, sems = take(4)
        kept = take(1)[0] if own else None
        scale_left = scale_right if own else scale_left
    else:
        sums_out, power_out, edge_out = take(3)

    power, edge = [], []
    for s in range(stations):
        h, place = place_of(s, stations)
        body = 2 * pieces_of(stations)[h][1] * windows * rows
        cells = []
        lines = []
        for k in range(chunks):
            chunk = right[k * parts + h]
            for w in range(windows):
                at = 2 * (place * windows + w)
                cell = chunk[pl.ds(at * rows, 2 * rows), :].astype(jnp.float32)
                cell = cell * cell
                cells.append(cell[:rows] + cell[rows:])
            line = chunk[pl.ds(body + 2 * place * windows, 2 * windows), :]
            line = line.astype(jnp.float32)
            lines.append(jnp.sum(line * line, axis=0, keepdims=True))
        power.append(sum(cells[1:], cells[0]))
        edge.append(sum(lines[1:], lines[0]))
    power, edge = jnp.concatenate(power, axis=0), jnp.concatenate(edge, axis=0)
    if not first:
        power, edge = power + power_in[...], edge + edge_in[...]
    if last:
        scale_right[...] = scales_of(power, edge, gain[...], window[...], stations, rows, total)
    else:
        power_out[...], edge_out[...] = power, edge

    step = min(16, rows)
    steps = rows // step

    def stored(e, i):
        return pltpu.make_async_copy(ready.at[e, i], out.at[e, i], sems.at[e, i])

    def tree(terms):
        while len(terms) > 1:
            terms = [x + y for x, y in zip(terms[::2], terms[1::2])] + (
                terms[-1:] if len(terms) % 2 else []
            )
        return terms[0].astype(jnp.float32)

    for i in range(stations):

        def turn(index, carry, i=i):
            q = pl.multiple_of(index * step, step)
            real, imag = [None] * stations, [None] * stations

            def cell(pieces, k, s, w, e):
                h, place = place_of(s, stations)
                at = ((place * windows + w) * 2 + e) * rows
                return pieces[k * parts + h][pl.ds(pl.multiple_of(at + q, step), step), :]

            for k in range(chunks):
                a = [cell(left, k, i, w, 0) for w in range(windows)]
                b = [cell(left, k, i, w, 1) for w in range(windows)]
                for j in range(i if own else 0, stations):
                    c = [cell(right, k, j, w, 0) for w in range(windows)]
                    d = [cell(right, k, j, w, 1) for w in range(windows)]
                    re = tree([a[w] * c[w] + b[w] * d[w] for w in range(windows)])
                    im = tree([b[w] * c[w] - a[w] * d[w] for w in range(windows)])
                    real[j] = re if k == 0 else real[j] + re
                    imag[j] = im if k == 0 else imag[j] + im
            if last:
                here = scale_left[pl.ds(pl.multiple_of(i * rows + q, step), step), :]
                here = here * (1.0 / total)
            for j in range(stations):
                to = pl.ds(q, step)
                if own and j < i:
                    if not last:
                        continue
                    real[j], imag[j] = kept[0, j, i, to, :], -kept[1, j, i, to, :]
                elif not first:
                    real[j] = real[j] + sums[0, i, j, to, :]
                    imag[j] = imag[j] + sums[1, i, j, to, :]
                if own and last and j > i:
                    kept[0, i, j, to, :], kept[1, i, j, to, :] = real[j], imag[j]
                if last:
                    there = scale_right[pl.ds(pl.multiple_of(j * rows + q, step), step), :]
                    to = pl.ds(q * stations + j, step, stride=stations)
                    board[0, to, :] = real[j] * (here * there)
                    board[1, to, :] = imag[j] * (here * there)
                else:
                    sums_out[0, i, j, to, :] = real[j]
                    sums_out[1, i, j, to, :] = imag[j]
            return carry

        lax.fori_loop(0, steps, turn, 0, unroll=True)
        if last:
            ready[:, i] = board[...].astype(jnp.bfloat16)
            for e in range(2):
                stored(e, i).start()
    if last:
        for i in range(stations):
            for e in range(2):
                stored(e, i).wait()


def cross(left, right, stations, windows, total, before=None, ends=None):
    own = right is None
    first, last = before is None, ends is not None
    chunks = len(left)
    height = sum(piece.shape[0] for piece in left[0])
    rows = height // (2 * stations * windows) - 1
    vmem = pl.BlockSpec(memory_space=pltpu.VMEM)
    shape = (2, stations, rows * stations, ROOT)
    scales = (stations * rows, ROOT)
    args = [piece for chunk in (*left, *(right or ())) for piece in chunk]
    args += [*(before or ()), *(ends or ())]
    args = [pltpu.with_memory_space_constraint(c, pltpu.VMEM) for c in args]
    if last:
        outs = [jax.ShapeDtypeStruct(shape, jnp.bfloat16)]
        out_specs = [pl.BlockSpec(memory_space=pl.ANY)]
        scratch = [
            pltpu.VMEM((2, *shape[2:]), jnp.float32),
            pltpu.VMEM(shape, jnp.bfloat16),
            pltpu.SemaphoreType.DMA((2, stations)),
        ]
        if own:
            outs.append(pltpu.VMEM(scales, jnp.float32))
            out_specs.append(vmem)
            scratch.append(pltpu.VMEM((2, stations, stations, rows, ROOT), jnp.float32))
        else:
            scratch.insert(0, pltpu.VMEM(scales, jnp.float32))
    else:
        outs = [
            pltpu.VMEM((2, stations, stations, rows, ROOT), jnp.float32),
            pltpu.VMEM(scales, jnp.float32),
            pltpu.VMEM((stations, ROOT), jnp.float32),
        ]
        out_specs = [vmem] * 3
        scratch = []
    result = pl.pallas_call(
        functools.partial(
            cross_kernel, stations=stations, windows=windows, rows=rows, chunks=chunks,
            total=total, own=own, first=first, last=last,
        ),
        out_shape=outs,
        in_specs=[vmem] * len(args),
        out_specs=out_specs,
        scratch_shapes=scratch,
    )(*args)
    if not last:
        return result
    spread = result[0].reshape(2, stations, rows, stations, ROOT).transpose(0, 1, 3, 2, 4)
    spread = spread.reshape(2, stations, stations, rows * ROOT)
    return (spread, result[1]) if own else spread


def brought(block, axis, distance):
    count = lax.axis_size(axis)
    return lax.ppermute(block, axis, [((i + distance) % count, i) for i in range(count)])


def program(traces, live_flag, response):
    stations, windows, _ = traces.shape
    bands, parts = lax.axis_size("band"), len(pieces_of(stations))
    band = lax.axis_index("band").astype(jnp.int32)
    blocks = lax.axis_size("sta")
    offset = blocks // 8
    total = live_flag.shape[1]
    split = transform(traces, live_flag, bands)
    even = lax.rem(lax.div(lax.axis_index("sta"), offset), 2) == 0
    relay = [(i, i + offset if i // offset % 2 == 0 else i - offset) for i in range(blocks)]

    def sent(k, h):
        pieces = [split[b][h] for b in range(bands)]
        if bands == 2:
            return jnp.where(band == k, *pieces)
        return lax.select_n((band + k) % bands, *pieces) if bands > 1 else pieces[0]

    mine, far, near = ([[] for _ in range(bands)] for _ in range(3))
    order = [(k, h, f"{min(k, 1)}_{h}") for k in range(bands) for h in range(parts)]
    for k, h, tag in order:
        mine[k].append(brought(sent(k, h), "band", -k) if k else sent(k, h))
    for k, h, tag in order:
        far[k].append(brought(mine[k][h], "sta", 2 * offset))
        if tag in DIRECT:
            near[k].append(brought(mine[k][h], "sta", offset))
        else:
            held = jnp.where(even, far[k][h], mine[k][h])
            near[k].append(lax.ppermute(held, "sta", relay))
    ends = [response.reshape(-1, ROOT), smoother()]

    def summed(theirs):
        return cross(mine[:1], theirs, stations, windows, total) if bands > 1 else None

    def ended(theirs, before):
        rest = slice(1 if before else 0, None)
        theirs = theirs and theirs[rest]
        return cross(mine[rest], theirs, stations, windows, total, before=before, ends=ends)

    sums = summed(None)
    own_cross, scale = ended(None, sums)
    ends.append(scale)
    far_cross = ended(far, summed(far[:1]))
    near_cross = ended(near, summed(near[:1]))
    return own_cross, near_cross, far_cross


def solution(mesh):
    in_specs = (P("sta", "band", None), P("sta", None), P("band"))
    out_specs = (P(None, "sta", None, "band"),) * 3
    return jax.shard_map(program, mesh=mesh, in_specs=in_specs, out_specs=out_specs, check_vma=False)
```
